256 devices in a mesh: leaf: 64 (over x, z, core), front: 4 (over y).
Axes of the slice: x: 4, y: 4, z: 8, core: 2. Of those that a mesh axis runs over, the one named last changes fastest.
Arguments:
- leaf_update: float32 [65536, 1024], P('leaf'), as said below
- separator_rows_1: float32 [16384, 1536], P(('leaf', 'front')), as said below
- remaining_rows_1: float32 [32768, 1536], P(('leaf', 'front'))
- separator_rows_2: float32 [8192, 1536], P(('leaf', 'front')), as said below
- remaining_rows_2: float32 [16384, 1536], P(('leaf', 'front'))
- separator_rows_3: float32 [4096, 1536], P(('leaf', 'front')), as said below
- remaining_rows_3: float32 [8192, 1536], P(('leaf', 'front'))
- child_map_1: int32 [64, 8], replicated, may hold values from 0 to 11, as said below
- child_map_2: int32 [32, 8], replicated, may hold values from 0 to 11, as said below
- child_map_3: int32 [16, 8], replicated, may hold values from 0 to 11, as said below
Outputs:
- pivot_factor_1: float32 [16384, 512], P(('leaf', 'front'))
- below_factor_1: float32 [32768, 512], P(('leaf', 'front'))
- pivot_factor_2: float32 [8192, 512], P(('leaf', 'front'))
- below_factor_2: float32 [16384, 512], P(('leaf', 'front'))
- pivot_factor_3: float32 [4096, 512], P(('leaf', 'front'))
- below_factor_3: float32 [8192, 512], P(('leaf', 'front'))
The draws below stay inside these ranges and needn't reach their ends.
Inputs may be any that keep to these rules, and one draw needn't show every extreme that they name: `child_map_1`: each row lists 8 distinct parent tiles in increasing order, the last one always 12 - 1. `child_map_2`: each row lists 8 distinct parent tiles in increasing order, the last one always 12 - 1. `child_map_3`: each row lists 8 distinct parent tiles in increasing order, the last one always 12 - 1. `leaf_update`: each block is symmetric positive definite, diagonal between 0.5 and 2, off-diagonal entries of magnitude about 0.008, smallest eigenvalue about 0.1 or more. Each front, separator_rows_1 above remaining_rows_1, is symmetric positive definite, diagonal between 2 and 4, off-diagonal entries of magnitude about 0.03, smallest eigenvalue about 0.35 or more. Each front, separator_rows_2 above remaining_rows_2, is symmetric positive definite, diagonal between 2 and 4, off-diagonal entries of magnitude about 0.03, smallest eigenvalue about 0.35 or more. Each front, separator_rows_3 above remaining_rows_3, is symmetric positive definite, diagonal between 2 and 4, off-diagonal entries of magnitude about 0.03, smallest eigenvalue about 0.35 or more.
All inputs are finite; a program needn't handle non-finite values.
Results may differ from the reference program's by a relative error of at most 0.0003.
Values sent between devices are 32-bit elements; how exact they have to be, the bound alone decides.
No kernel may reach another device: no remote copies, remote signals or barrier semaphores. Data moves between devices by JAX's collectives and lax.ppermute only.
A program may use at most 128 MiB of HBM per device.

```python
import jax
import jax.numpy as jnp
from jax import lax

TILE = 128
SEP = 512
UPD = 1024
NF = 1536
NT = 12
UT = 8
N_LEAF = 64


def symmetric_fronts(key, front_total, order_size, spread, diag_low, diag_high):
    noise_key, diag_key, sign_key = jax.random.split(key, 3)
    noise_all = jax.random.normal(noise_key, (front_total, order_size, order_size), jnp.float32)
    diag_values = jax.random.uniform(diag_key, (front_total, order_size), jnp.float32, diag_low, diag_high)
    sign_draw = jax.random.randint(sign_key, (front_total, order_size), 0, 2)
    signs = (2 * sign_draw - 1).astype(jnp.float32)
    mirrored = (noise_all + jnp.swapaxes(noise_all, 1, 2)) * (spread * 0.70710678)
    coupled = mirrored + spread * signs[:, :, None] * signs[:, None, :]
    eye_mask = jnp.eye(order_size, dtype=jnp.float32)
    return coupled * (1.0 - eye_mask) + diag_values[:, :, None] * eye_mask


def draw_tile_map(key, row_total):
    random_bits = jax.random.randint(key, (row_total, NT - 1), 0, 1 << 20)
    scores = random_bits * NT + jnp.arange(NT - 1, dtype=jnp.int32)[None, :]
    picked = jnp.argsort(scores, axis=1)[:, :UT - 1]
    chosen = jnp.sort(picked, axis=1)
    last_tile = jnp.full((row_total, 1), NT - 1, dtype=jnp.int32)
    return jnp.concatenate([chosen.astype(jnp.int32), last_tile], axis=1).astype(jnp.int32)


def draw_leaf_update(key, part):
    fronts = symmetric_fronts(jax.random.fold_in(key, 21), N_LEAF, UPD, 0.006, 0.5, 2.0)
    return fronts.reshape(N_LEAF * UPD, UPD)


def draw_separator_rows_1(key, part):
    fronts = symmetric_fronts(jax.random.fold_in(key, 31), N_LEAF // 2, NF, 0.02, 2.0, 4.0)
    return fronts[:, :SEP].reshape(-1, NF)


def draw_remaining_rows_1(key, part):
    fronts = symmetric_fronts(jax.random.fold_in(key, 31), N_LEAF // 2, NF, 0.02, 2.0, 4.0)
    return fronts[:, SEP:].reshape(-1, NF)


def draw_separator_rows_2(key, part):
    fronts = symmetric_fronts(jax.random.fold_in(key, 32), N_LEAF // 4, NF, 0.02, 2.0, 4.0)
    return fronts[:, :SEP].reshape(-1, NF)


def draw_remaining_rows_2(key, part):
    fronts = symmetric_fronts(jax.random.fold_in(key, 32), N_LEAF // 4, NF, 0.02, 2.0, 4.0)
    return fronts[:, SEP:].reshape(-1, NF)


def draw_separator_rows_3(key, part):
    fronts = symmetric_fronts(jax.random.fold_in(key, 33), N_LEAF // 8, NF, 0.02, 2.0, 4.0)
    return fronts[:, :SEP].reshape(-1, NF)


def draw_remaining_rows_3(key, part):
    fronts = symmetric_fronts(jax.random.fold_in(key, 33), N_LEAF // 8, NF, 0.02, 2.0, 4.0)
    return fronts[:, SEP:].reshape(-1, NF)


def draw_child_map_1(key, part):
    return draw_tile_map(jax.random.fold_in(key, 41), N_LEAF)


def draw_child_map_2(key, part):
    return draw_tile_map(jax.random.fold_in(key, 42), N_LEAF // 2)


def draw_child_map_3(key, part):
    return draw_tile_map(jax.random.fold_in(key, 43), N_LEAF // 4)


def setup_inputs(seed: int = 0) -> dict:
    arg_keys = jax.random.split(jax.random.key(seed), 11)
    return {
        "leaf_update": draw_leaf_update(jax.random.fold_in(arg_keys[10], 71), 0),
        "separator_rows_1": draw_separator_rows_1(jax.random.fold_in(arg_keys[10], 71), 0),
        "remaining_rows_1": draw_remaining_rows_1(jax.random.fold_in(arg_keys[10], 71), 0),
        "separator_rows_2": draw_separator_rows_2(jax.random.fold_in(arg_keys[10], 71), 0),
        "remaining_rows_2": draw_remaining_rows_2(jax.random.fold_in(arg_keys[10], 71), 0),
        "separator_rows_3": draw_separator_rows_3(jax.random.fold_in(arg_keys[10], 71), 0),
        "remaining_rows_3": draw_remaining_rows_3(jax.random.fold_in(arg_keys[10], 71), 0),
        "child_map_1": draw_child_map_1(jax.random.fold_in(arg_keys[10], 71), 0),
        "child_map_2": draw_child_map_2(jax.random.fold_in(arg_keys[10], 71), 0),
        "child_map_3": draw_child_map_3(jax.random.fold_in(arg_keys[10], 71), 0),
    }


def tile_rows(tile_map):
    offsets = jnp.arange(TILE, dtype=jnp.int32)
    return (tile_map[:, None].astype(jnp.int32) * TILE + offsets[None, :]).reshape(-1).astype(jnp.int32)

def factor_front(sep_part, upd_part, first_child, second_child, first_map, second_map, with_update):
    front_full = jnp.concatenate([sep_part, upd_part], axis=0)
    for child_block, tile_map in ((first_child, first_map), (second_child, second_map)):
        index_list = tile_rows(tile_map)
        front_full = front_full.at[index_list[:, None], index_list[None, :]].add(child_block)
    diag_factor = jnp.linalg.cholesky(front_full[:SEP, :SEP])
    solved = lax.linalg.triangular_solve(diag_factor, front_full[SEP:, :SEP], left_side=False, lower=True, transpose_a=True)
    if with_update:
        update = front_full[SEP:, SEP:] - jnp.dot(solved, solved.T, precision=lax.Precision.HIGHEST)
        return (diag_factor, solved, update)
    return (diag_factor, solved)

def reference(leaf_update, separator_rows_1, remaining_rows_1, separator_rows_2, remaining_rows_2, separator_rows_3, remaining_rows_3, child_map_1, child_map_2, child_map_3):
    children = leaf_update.reshape(N_LEAF, UPD, UPD)
    sections = ((separator_rows_1, remaining_rows_1, child_map_1), (separator_rows_2, remaining_rows_2, child_map_2), (separator_rows_3, remaining_rows_3, child_map_3))
    outputs = []
    for section_number in range(1, 4):
        sep_all, upd_all, map_all = sections[section_number - 1]
        front_total = N_LEAF // 2 ** section_number
        with_update = section_number < 3

        def one_front(packed, with_update=with_update):
            sep_part, upd_part, pair_block, pair_maps = packed
            return factor_front(sep_part, upd_part, pair_block[0], pair_block[1], pair_maps[0], pair_maps[1], with_update)
        factors = lax.map(one_front, (sep_all.reshape(front_total, SEP, NF), upd_all.reshape(front_total, UPD, NF), children.reshape(front_total, 2, UPD, UPD), map_all.reshape(front_total, 2, UT)))
        outputs.append(factors[0].reshape(front_total * SEP, SEP))
        outputs.append(factors[1].reshape(front_total * UPD, SEP))
        if with_update:
            children = factors[2]
    return (outputs[0], outputs[1], outputs[2], outputs[3], outputs[4], outputs[5])
```

```python
import functools
import jax
import jax.numpy as jnp
from jax import lax
from jax.experimental import pallas as pl
from jax.experimental.pallas import tpu as pltpu
from jax.sharding import PartitionSpec as P

TILE = 128
SEP = 512
UPD = 1024
F32 = jnp.float32
BF16 = jnp.bfloat16
VM = pltpu.VMEM
ROWS = (((1,), (1,)), ((), ()))


def params():
    return pltpu.CompilerParams(vmem_limit_bytes=56 << 20)


def cost(us):
    return pl.CostEstimate(flops=int(us * 1e9), bytes_accessed=int(us * 3e6), transcendentals=0)


def split(a):
    high = a.astype(BF16)
    return high, (a - high.astype(F32)).astype(BF16)


def dot_split(a, b):
    ah, al = a
    bh, bl = b
    mul = lambda x, y: lax.dot_general(x, y, ROWS, preferred_element_type=F32)
    return mul(ah, bh) + (mul(ah, bl) + mul(al, bh))


def dot_rows(a, b):
    return dot_split(split(a), split(b))


def lane(x, c):
    return jnp.broadcast_to(x[:, c : c + 1], (8, TILE))


def sublane(x, r):
    return jnp.broadcast_to(x[r : r + 1, :], (8, TILE))


def factor_tile(d_ref, w_ref):
    rows8 = lax.broadcasted_iota(jnp.int32, (8, TILE), 0)
    ri = lax.broadcasted_iota(jnp.int32, (TILE, TILE), 0)
    ci = lax.broadcasted_iota(jnp.int32, (TILE, TILE), 1)
    w_ref[...] = jnp.where(ri == ci, 1.0, 0.0).astype(F32)
    for q in range(16):
        o = 8 * q
        rows, inv = d_ref[o : o + 8, :], w_ref[o : o + 8, :]
        cols = [lane(rows, o + t) for t in range(8)]
        a = [[None] * 8 for _ in range(8)]
        for t in range(8):
            for s in range(t, 8):
                a[s][t] = sublane(cols[t], s)
        rs = [None] * 8
        low = [[None] * 8 for _ in range(8)]
        x_rows = [None] * 8
        v_rows = [None] * 8
        for t in range(8):
            rs[t] = lax.rsqrt(a[t][t])
            for s in range(t + 1, 8):
                low[s][t] = a[s][t] * rs[t]
            for s in range(t + 1, 8):
                for u in range(t + 1, s + 1):
                    a[s][u] = a[s][u] - low[s][t] * low[u][t]
            x, v = sublane(rows, t), sublane(inv, t)
            for u in range(t):
                x = x - low[t][u] * x_rows[u]
                v = v - low[t][u] * v_rows[u]
            x_rows[t] = x * rs[t]
            v_rows[t] = v * rs[t]
        packed = v_rows[0]
        for t in range(1, 8):
            packed = jnp.where(rows8 == t, v_rows[t], packed)
        w_ref[o : o + 8, :] = packed
        for p in range(q + 1, 16):
            po = 8 * p
            d_rows, w_rows = d_ref[po : po + 8, :], w_ref[po : po + 8, :]
            coef = [None] * 8
            for t in range(8):
                c = lane(d_rows, o + t)
                for u in range(t):
                    c = c - coef[u] * low[t][u]
                coef[t] = c * rs[t]
            for t in range(8):
                d_rows = d_rows - coef[t] * x_rows[t]
                w_rows = w_rows - coef[t] * v_rows[t]
            d_ref[po : po + 8, :] = d_rows
            w_ref[po : po + 8, :] = w_rows


def places():
    return lax.axis_index("leaf"), lax.axis_index("front")


def tile_place(k):
    r = jnp.int32(0)
    for start in (1, 3, 6, 10, 15, 21, 28):
        r = r + (k >= start).astype(jnp.int32)
    return r, k - lax.div(r * (r + 1), 2)


def block(i):
    return pl.ds(pl.multiple_of(i * TILE, TILE), TILE)


def scatter(dst_ref, maps_ref, child, get_tile, count, first, row_lo, row_n, col_lo, col_n):
    def step(i, carry):
        r, c = tile_place(first + i)
        mi = maps_ref[child, r] - row_lo
        mj = maps_ref[child, c] - col_lo

        @pl.when((mi >= 0) & (mi < row_n) & (mj >= 0) & (mj < col_n))
        def _():
            dst_ref[block(mi), block(mj)] += get_tile(i, r, c)

        return carry

    lax.fori_loop(0, count, step, 0)


def pivot_kernel(level, n_pieces, maps_ref, *refs):
    pieces = refs[:n_pieces]
    tiles = refs[n_pieces : len(refs) - 6]
    l_ref, t_ref, own_ref, f, d, w = refs[len(refs) - 6 :]
    leaf, y = places()
    core = leaf & 1
    n = SEP // (4 * 2**level)
    rels = (0, 3, 1, 2)

    def put(ref, start, ly, y_rel):
        pos = (ly & (2**level - 1)) * 4 + ((y + y_rel) & 3)
        f[pl.ds(pl.multiple_of(pos * n, n), n), :] = ref[start : start + n, :]

    def put_group(ref, start, core_rel, y_rel):
        if level == 1:
            put(ref, start, leaf ^ core_rel, y_rel)
            return
        for z1 in range(2):
            base = start + 64 * z1
            who = leaf ^ core_rel ^ (z1 << 1)
            if level == 2:
                put(ref, base, who, y_rel)
            else:
                for z2 in range(2):
                    put(ref, base + 32 + 16 * z2, who ^ (z2 << 2), y_rel)

    size = 64 if level == 1 else 128
    for i, rel in enumerate(rels):
        put_group(pieces[i], 0, 0, rel)
        put_group(pieces[4], i * size, 1, rel)

    own = leaf >> (level - 1)
    sib = own ^ 1
    if level == 1:
        for child, ref in ((own, tiles[0]), (sib, tiles[1])):
            scatter(f, maps_ref, child, lambda i, r, c, ref=ref: ref[block(r), block(c)], 10, 0, 0, 4, 0, 4)
    else:
        own10, half_a, half_b = tiles
        scatter(f, maps_ref, own, lambda i, r, c: own10[i], 10, 0, 0, 4, 0, 4)
        scatter(f, maps_ref, sib, lambda i, r, c: half_a[i], 5, core * 5, 0, 4, 0, 4)
        scatter(f, maps_ref, sib, lambda i, r, c: half_b[i], 5, (1 - core) * 5, 0, 4, 0, 4)

    ri = lax.broadcasted_iota(jnp.int32, (SEP, TILE), 0)
    ci = lax.broadcasted_iota(jnp.int32, (SEP, TILE), 1)

    def step(b, carry):
        d[...] = f[block(b), block(b)]
        factor_tile(d, w)
        t_ref[b] = w[...]
        panel = dot_rows(f[:, block(b)], w[...])
        panel = jnp.where(ri - b * TILE >= ci, panel, 0.0)
        l_ref[:, block(b)] = panel
        f[...] = f[...] - dot_rows(panel, panel)
        return carry

    lax.fori_loop(0, 4, step, 0)
    pos = (leaf & (2**level - 1)) * 4 + y
    own_ref[...] = l_ref[pl.ds(pl.multiple_of(pos * n, n), n), :]


def vspec(shape):
    nd = len(shape)
    return pl.BlockSpec(shape, lambda i: (0,) * nd)


def pivot(level, maps, pieces, tiles, tile_shapes):
    n = SEP // (4 * 2**level)
    size = 64 if level == 1 else 128
    piece_specs = [vspec((size, SEP))] * 4 + [vspec((4 * size, SEP))]
    return pl.pallas_call(
        functools.partial(pivot_kernel, level, 5),
        grid=(1,),
        in_specs=[pl.BlockSpec(memory_space=pltpu.SMEM)] + piece_specs + [vspec(s) for s in tile_shapes],
        out_specs=[vspec((SEP, SEP)), vspec((4, TILE, TILE)), vspec((n, SEP))],
        out_shape=[
            jax.ShapeDtypeStruct((SEP, SEP), F32),
            jax.ShapeDtypeStruct((4, TILE, TILE), F32),
            jax.ShapeDtypeStruct((n, SEP), F32),
        ],
        scratch_shapes=[VM((SEP, SEP), F32), VM((TILE, TILE), F32), VM((TILE, TILE), F32)],
        compiler_params=params(),
        cost_estimate=cost(25),
        name="pivot%d" % level,
    )(maps, *pieces, *tiles)


def solve_rows(x, l_ref, t_ref, out_ref):
    done = None
    for b in range(4):
        cols = x[:, b * TILE : (b + 1) * TILE]
        if b:
            lb = split(l_ref[b * TILE : (b + 1) * TILE, : b * TILE])
            cols = cols - dot_split((done[0], done[1]), lb)
        part = dot_rows(cols, t_ref[b])
        out_ref[:, b * TILE : (b + 1) * TILE] = part
        ph, plo = split(part)
        done = (ph, plo) if done is None else (
            jnp.concatenate([done[0], ph], axis=1),
            jnp.concatenate([done[1], plo], axis=1),
        )
    return done


def spread_kernel(maps_ref, own_ref, sib11_ref, sibr_ref, a21, a22, b21, b22):
    leaf, _ = places()
    for ref in (a21, a22, b21, b22):
        ref[...] = jnp.zeros_like(ref)
    own, sib = leaf, leaf ^ 1
    get_own = lambda i, r, c: own_ref[block(r), block(c)]
    get_sib = lambda i, r, c: sibr_ref[block(r - 4), block(c)]
    get_s11 = lambda i, r, c: sib11_ref[block(r), block(c)]
    for dst, lo, clo, cn in ((a21, 4, 0, 4), (a22, 4, 4, 4), (b21, 8, 0, 4), (b22, 8, 4, 8)):
        top = lo == 4
        scatter(dst, maps_ref, own, get_own, 28 if top else 26, 0 if top else 10, lo, 4, clo, cn)
        if top:
            scatter(dst, maps_ref, sib, get_s11, 10, 0, lo, 4, clo, cn)
        scatter(dst, maps_ref, sib, get_sib, 18 if top else 26, 10, lo, 4, clo, cn)


def spread(maps, own, sib11, sibr):
    shapes = [(SEP, SEP), (SEP, SEP), (SEP, SEP), (SEP, UPD)]
    return pl.pallas_call(
        spread_kernel,
        grid=(1,),
        in_specs=[pl.BlockSpec(memory_space=pltpu.SMEM), vspec((UPD, UPD)), vspec((SEP, SEP)), vspec((SEP, UPD))],
        out_specs=[vspec(s) for s in shapes],
        out_shape=[jax.ShapeDtypeStruct(s, F32) for s in shapes],
        compiler_params=params(),
        cost_estimate=cost(8),
        name="spread",
    )(maps, own, sib11, sibr)


def fetch(copies):
    for c in copies:
        c.start()


def finish(copies):
    for c in copies:
        c.wait()


def upper_kernel_1(l_ref, t_ref, s21, s22, g_own, g_sw, l21_ref, u_ref, half_ref, e, sem):
    leaf, _ = places()
    core = leaf & 1

    @pl.when(core == 0)
    def _():
        pltpu.make_async_copy(g_own.at[:, :, pl.ds(0, UPD)], e, sem).start()

    @pl.when(core == 1)
    def _():
        pltpu.make_async_copy(g_sw.at[:, :, pl.ds(0, UPD)], e, sem).start()

    pltpu.make_async_copy(g_own.at[:, :, pl.ds(0, UPD)], e, sem).wait()
    full = e[...].reshape(SEP, UPD)
    done = solve_rows(s21[...] + full[:, :SEP], l_ref, t_ref, l21_ref)
    emit_upper(done, s22[...] + full[:, SEP:], u_ref, half_ref, core)


def emit_upper(done, f22, u_ref, half_ref, core):
    k = 0
    for i in range(4):
        rows = slice(i * TILE, (i + 1) * TILE)
        wide = (i + 1) * TILE
        prod = dot_split((done[0][rows], done[1][rows]), (done[0][:wide], done[1][:wide]))
        out = f22[rows, :wide] - prod
        for j in range(i + 1):
            u_ref[k] = out[:, j * TILE : (j + 1) * TILE]
            k += 1

    half_ref[...] = u_ref[pl.ds(core * 5, 5)]


def upper_1(lfac, tinv, s21, s22, g_own, g_sw):
    return pl.pallas_call(
        upper_kernel_1,
        grid=(1,),
        in_specs=[vspec((SEP, SEP)), vspec((4, TILE, TILE)), vspec((SEP, SEP)), vspec((SEP, SEP))]
        + [pl.BlockSpec(memory_space=pl.ANY)] * 2,
        out_specs=[vspec((SEP, SEP)), vspec((10, TILE, TILE)), vspec((5, TILE, TILE))],
        out_shape=[
            jax.ShapeDtypeStruct((SEP, SEP), F32),
            jax.ShapeDtypeStruct((10, TILE, TILE), F32),
            jax.ShapeDtypeStruct((5, TILE, TILE), F32),
        ],
        scratch_shapes=[VM((4, TILE, UPD), F32), pltpu.SemaphoreType.DMA],
        compiler_params=params(),
        cost_estimate=cost(5),
        name="upper1",
    )(lfac, tinv, s21, s22, g_own, g_sw)


def lower_kernel_1(l_ref, t_ref, s21, s22, l21a, g_own, g_sw, u_ref, half_ref, below_ref, e, l21b, sem):
    leaf, y = places()
    core = leaf & 1

    @pl.when(core == 1)
    def _():
        pltpu.make_async_copy(g_own, e, sem).start()

    @pl.when(core == 0)
    def _():
        pltpu.make_async_copy(g_sw, e, sem).start()

    pltpu.make_async_copy(g_own, e, sem).wait()
    full = e[...].reshape(SEP, SEP + UPD)
    done = solve_rows(s21[...] + full[:, :SEP], l_ref, t_ref, l21b)
    top = split(l21a[...])
    f22 = s22[...] + full[:, SEP:]
    k = 0
    for i in range(4):
        rows = slice(i * TILE, (i + 1) * TILE)
        wide = (i + 1) * TILE
        left = (done[0][rows], done[1][rows])
        out = f22[rows, :SEP] - dot_split(left, top)
        for j in range(4):
            u_ref[k] = out[:, j * TILE : (j + 1) * TILE]
            k += 1
        out = f22[rows, SEP : SEP + wide] - dot_split(left, (done[0][:wide], done[1][:wide]))
        for j in range(i + 1):
            u_ref[k] = out[:, j * TILE : (j + 1) * TILE]
            k += 1
    half_ref[...] = u_ref[pl.ds(core * 13, 13)]

    @pl.when(core == 0)
    def _():
        below_ref[...] = l21a[block(y), :]

    @pl.when(core == 1)
    def _():
        below_ref[...] = l21b[block(y), :]


def lower_1(lfac, tinv, s21, s22, l21a, g_own, g_sw):
    return pl.pallas_call(
        lower_kernel_1,
        grid=(1,),
        in_specs=[vspec((SEP, SEP)), vspec((4, TILE, TILE)), vspec((SEP, SEP)), vspec((SEP, UPD)), vspec((SEP, SEP))]
        + [pl.BlockSpec(memory_space=pl.ANY)] * 2,
        out_specs=[vspec((26, TILE, TILE)), vspec((13, TILE, TILE)), vspec((TILE, SEP))],
        out_shape=[
            jax.ShapeDtypeStruct((26, TILE, TILE), F32),
            jax.ShapeDtypeStruct((13, TILE, TILE), F32),
            jax.ShapeDtypeStruct((TILE, SEP), F32),
        ],
        scratch_shapes=[VM((4, TILE, SEP + UPD), F32), VM((SEP, SEP), F32), pltpu.SemaphoreType.DMA],
        compiler_params=params(),
        cost_estimate=cost(8),
        name="lower1",
    )(lfac, tinv, s21, s22, l21a, g_own, g_sw)


def load_level_2(which, g_own, g_sw, e, sem):
    leaf, _ = places()
    core = leaf & 1
    z_rel = ((leaf >> 1) & 1) ^ which
    copies = []
    for y in range(4):
        for part in range(2):
            for src, who in ((g_own, core), (g_sw, 1 - core)):
                row = pl.multiple_of(who * 256 + y * 64, 64)
                copies.append(
                    pltpu.make_async_copy(
                        src.at[y, z_rel, part], e.at[part, pl.ds(row, 64), :], sem.at[len(copies)]
                    )
                )
    return copies


def scatter_level_2(e, maps_ref, leaf, core, own10, own26, ha10, hb10, ha26, hb26, row_lo):
    own = leaf >> 1
    sib = own ^ 1
    for part in range(2):
        dst = e.at[part]
        args = (row_lo, 4, 4 * part, 4)
        if row_lo == 4:
            scatter(dst, maps_ref, own, lambda i, r, c: own10[i], 10, 0, *args)
            scatter(dst, maps_ref, sib, lambda i, r, c: ha10[i], 5, core * 5, *args)
            scatter(dst, maps_ref, sib, lambda i, r, c: hb10[i], 5, (1 - core) * 5, *args)
        scatter(dst, maps_ref, own, lambda i, r, c: own26[i], 26, 10, *args)
        scatter(dst, maps_ref, sib, lambda i, r, c: ha26[i], 13, 10 + core * 13, *args)
        scatter(dst, maps_ref, sib, lambda i, r, c: hb26[i], 13, 10 + (1 - core) * 13, *args)


def upper_kernel_2(maps_ref, l_ref, t_ref, own10, own26, ha10, hb10, ha26, hb26, g_own, g_sw,
                   l21_ref, u_ref, half_ref, e, sem):
    leaf, _ = places()
    core = leaf & 1
    copies = load_level_2(0, g_own, g_sw, e, sem)
    fetch(copies)
    finish(copies)
    scatter_level_2(e, maps_ref, leaf, core, own10, own26, ha10, hb10, ha26, hb26, 4)
    done = solve_rows(e[0], l_ref, t_ref, l21_ref)
    emit_upper(done, e[1], u_ref, half_ref, core)


def upper_2(maps, lfac, tinv, tiles, g_own, g_sw):
    return pl.pallas_call(
        upper_kernel_2,
        grid=(1,),
        in_specs=[pl.BlockSpec(memory_space=pltpu.SMEM), vspec((SEP, SEP)), vspec((4, TILE, TILE))]
        + [vspec((n, TILE, TILE)) for n in (10, 26, 5, 5, 13, 13)]
        + [pl.BlockSpec(memory_space=pl.ANY)] * 2,
        out_specs=[vspec((SEP, SEP)), vspec((10, TILE, TILE)), vspec((5, TILE, TILE))],
        out_shape=[
            jax.ShapeDtypeStruct((SEP, SEP), F32),
            jax.ShapeDtypeStruct((10, TILE, TILE), F32),
            jax.ShapeDtypeStruct((5, TILE, TILE), F32),
        ],
        scratch_shapes=[VM((2, SEP, SEP), F32), pltpu.SemaphoreType.DMA((16,))],
        compiler_params=params(),
        cost_estimate=cost(7),
        name="upper2",
    )(maps, lfac, tinv, *tiles, g_own, g_sw)


def lower_kernel_2(maps_ref, maps3_ref, l_ref, t_ref, l21a, u10, own26, ha26, hb26, g_own, g_sw,
                   mine_ref, send_ref, below_ref, e, l21b, u21, sem):
    leaf, y = places()
    core = leaf & 1
    copies = load_level_2(1, g_own, g_sw, e, sem)
    fetch(copies)
    finish(copies)
    scatter_level_2(e, maps_ref, leaf, core, None, own26, None, None, ha26, hb26, 8)
    done = solve_rows(e[0], l_ref, t_ref, l21b)
    u21[...] = e[1] - dot_split(done, split(l21a[...]))
    child = leaf >> 2
    stripe = pl.ds(pl.multiple_of(y * 32, 32), 32)
    for out_ref, who in ((mine_ref, leaf), (send_ref, leaf ^ 4)):
        out_ref[...] = jnp.zeros_like(out_ref)
        want = 4 + (who & 7)
        for j in range(1, 8):
            @pl.when(maps3_ref[child, j] == want)
            def _(j=j, out_ref=out_ref):
                for c in range(min(j, 4)):
                    mj = maps3_ref[child, c]

                    @pl.when(mj < 4)
                    def _(c=c, mj=mj):
                        if j < 4:
                            piece = u10[j * (j + 1) // 2 + c, stripe, :]
                        else:
                            row = pl.multiple_of((j - 4) * TILE + y * 32, 32)
                            piece = u21[pl.ds(row, 32), c * TILE : (c + 1) * TILE]
                        out_ref[:, block(mj)] = piece

    pos = ((leaf & 3) * 4 + y) * 64

    @pl.when(pos < SEP)
    def _():
        below_ref[...] = l21a[pl.ds(pl.multiple_of(pos, 64), 64), :]

    @pl.when(pos >= SEP)
    def _():
        below_ref[...] = l21b[pl.ds(pl.multiple_of(pos - SEP, 64), 64), :]


def lower_2(maps, maps3, lfac, tinv, l21a, u10, tiles, g_own, g_sw):
    return pl.pallas_call(
        lower_kernel_2,
        grid=(1,),
        in_specs=[pl.BlockSpec(memory_space=pltpu.SMEM)] * 2
        + [vspec((SEP, SEP)), vspec((4, TILE, TILE)), vspec((SEP, SEP))]
        + [vspec((n, TILE, TILE)) for n in (10, 26, 13, 13)]
        + [pl.BlockSpec(memory_space=pl.ANY)] * 2,
        out_specs=[vspec((32, SEP)), vspec((32, SEP)), vspec((64, SEP))],
        out_shape=[
            jax.ShapeDtypeStruct((32, SEP), F32),
            jax.ShapeDtypeStruct((32, SEP), F32),
            jax.ShapeDtypeStruct((64, SEP), F32),
        ],
        scratch_shapes=[VM((2, SEP, SEP), F32), VM((SEP, SEP), F32), VM((SEP, SEP), F32), pltpu.SemaphoreType.DMA((16,))],
        compiler_params=params(),
        cost_estimate=cost(7),
        name="lower2",
    )(maps, maps3, lfac, tinv, l21a, u10, *tiles, g_own, g_sw)


def last_kernel(l_ref, t_ref, e_ref, mine_ref, got_ref, out_ref):
    solve_rows(e_ref[...] + mine_ref[...] + got_ref[...], l_ref, t_ref, out_ref)


def last(lfac, tinv, rem3, mine, got):
    return pl.pallas_call(
        last_kernel,
        grid=(1,),
        in_specs=[vspec((SEP, SEP)), vspec((4, TILE, TILE))] + [vspec((32, SEP))] * 3,
        out_specs=vspec((32, SEP)),
        out_shape=jax.ShapeDtypeStruct((32, SEP), F32),
        compiler_params=params(),
        cost_estimate=cost(3),
        name="last",
    )(lfac, tinv, rem3, mine, got)


def swap(x, bit):
    return lax.ppermute(x, "leaf", [(i, i ^ (1 << bit)) for i in range(lax.axis_size("leaf"))])


def shift(x, d):
    n = lax.axis_size("front")
    return lax.ppermute(x, "front", [(i, (i + d) % n) for i in range(n)])


def around(x):
    got = [x, shift(x, 1), shift(x, -1), shift(x, 2)]
    return got + [swap(jnp.concatenate(got, axis=0), 0)]


def after(x, *deps):
    return lax.optimization_barrier((x,) + deps)[0]


def body(leaf_update, sep1, rem1, sep2, rem2, sep3, rem3, map1, map2, map3):
    u_sib11 = swap(leaf_update[:SEP, :SEP], 0)
    u_sibr = swap(leaf_update[SEP:, :], 0)
    pieces1 = around(sep1[:, :SEP])
    g1 = lax.all_gather(rem1, "front", axis=0, tiled=False)

    s3 = sep3[:, :SEP]
    s3 = jnp.concatenate([sep2[:, :SEP], s3, swap(s3, 2)], axis=0)
    s3 = jnp.concatenate([s3, swap(s3, 1)], axis=0)
    s3 = after(s3, pieces1[1], pieces1[2], pieces1[3])
    pieces2 = around(s3)

    r2 = jnp.stack([rem2[:, :SEP], rem2[:, SEP:UPD]])
    r2 = jnp.stack([r2, swap(r2, 1)])

    a21, a22, b21, b22 = spread(map1, leaf_update, u_sib11, u_sibr)
    l1, t1, out_p1 = pivot(1, map1, pieces1, [leaf_update, u_sib11], [(SEP, SEP)] * 2)
    g1_sw = swap(g1, 0)
    g2 = lax.all_gather(after(r2, g1), "front", axis=0, tiled=False)
    l21a, u10, half10 = upper_1(l1, t1, a21, a22, g1, g1_sw)
    got10 = swap(half10, 1)
    u26, half26, out_b1 = lower_1(l1, t1, b21, b22, l21a, g1, g1_sw)
    got26 = swap(after(half26, got10), 1)
    sw10 = swap(got10, 0)
    l2, t2, out_p2 = pivot(2, map2, pieces2, [u10, got10, sw10], [(n, TILE, TILE) for n in (10, 5, 5)])
    g2_sw = swap(g2, 0)
    sw26 = swap(got26, 0)
    l21a, v10, half10 = upper_2(map2, l2, t2, [u10, u26, got10, sw10, got26, sw26], g2, g2_sw)
    got10 = swap(half10, 2)
    mine, send, out_b2 = lower_2(map2, map3, l2, t2, l21a, v10, [u26, got26, sw26], g2, g2_sw)
    got_rows = swap(send, 2)
    sw10 = swap(got10, 0)
    l3, t3, out_p3 = pivot(3, map3, pieces2, [v10, got10, sw10], [(n, TILE, TILE) for n in (10, 5, 5)])
    out_b3 = last(l3, t3, rem3, mine, got_rows)
    return out_p1, out_b1, out_p2, out_b2, out_p3, out_b3


def solution(mesh):
    both = P(("leaf", "front"), None)
    in_specs = (P("leaf", None),) + (both,) * 6 + (P(), P(), P())
    return jax.shard_map(body, mesh=mesh, in_specs=in_specs, out_specs=(both,) * 6, check_vma=False)
```

```python
import functools
import jax
import jax.numpy as jnp
from jax import lax
from jax.experimental import pallas as pl
from jax.experimental.pallas import tpu as pltpu
from jax.sharding import PartitionSpec as P

TILE = 128
SEP = 512
UPD = 1024
F32 = jnp.float32
BF16 = jnp.bfloat16
AHEAD = 3
HALF = SEP // 2
ANY = pl.BlockSpec(memory_space=pl.ANY)
SMEM = pl.BlockSpec(memory_space=pltpu.SMEM)
VM = pltpu.VMEM
ROWS = (((1,), (1,)), ((), ()))


def params():
    return pltpu.CompilerParams(vmem_limit_bytes=56 << 20)


def cost(us):
    return pl.CostEstimate(flops=int(us * 1e9), bytes_accessed=int(us * 3e6), transcendentals=0)


def split(a):
    high = a.astype(BF16)
    return high, (a - high.astype(F32)).astype(BF16)


def dot_split(a, b):
    ah, al = a
    bh, bl = b
    mul = lambda x, y: lax.dot_general(x, y, ROWS, preferred_element_type=F32)
    return mul(ah, bh) + (mul(ah, bl) + mul(al, bh))


def dot_rows(a, b):
    return dot_split(split(a), split(b))


def lane(x, c):
    return jnp.broadcast_to(x[:, c : c + 1], (8, TILE))


def sublane(x, r):
    return jnp.broadcast_to(x[r : r + 1, :], (8, TILE))


def factor_tile(d_ref, w_ref):
    rows8 = lax.broadcasted_iota(jnp.int32, (8, TILE), 0)
    ri = lax.broadcasted_iota(jnp.int32, (TILE, TILE), 0)
    ci = lax.broadcasted_iota(jnp.int32, (TILE, TILE), 1)
    w_ref[...] = jnp.where(ri == ci, 1.0, 0.0).astype(F32)

    def pack(parts):
        out = parts[0]
        for t in range(1, 8):
            out = jnp.where(rows8 == t, parts[t], out)
        return out

    for q in range(16):
        o = 8 * q
        rows, inv = d_ref[o : o + 8, :], w_ref[o : o + 8, :]
        cols = [lane(rows, o + t) for t in range(8)]
        a = [[None] * 8 for _ in range(8)]
        for t in range(8):
            for s in range(t, 8):
                a[s][t] = sublane(cols[t], s)
        rs = [None] * 8
        low = [[None] * 8 for _ in range(8)]
        x_rows = [None] * 8
        v_rows = [None] * 8
        for t in range(0, 8, 2):
            aa, bb, cc = a[t][t], a[t + 1][t], a[t + 1][t + 1]
            rs[t] = lax.rsqrt(aa)
            rs[t + 1] = lax.rsqrt(aa * cc - bb * bb) * (aa * rs[t])
            low[t + 1][t] = bb * rs[t]
            for s in range(t + 2, 8):
                low[s][t] = a[s][t] * rs[t]
                low[s][t + 1] = (a[s][t + 1] - low[s][t] * low[t + 1][t]) * rs[t + 1]
            for s in range(t + 2, 8):
                for u in range(t + 2, s + 1):
                    a[s][u] = (a[s][u] - low[s][t] * low[u][t]) - low[s][t + 1] * low[u][t + 1]
        for t in range(8):
            x, v = sublane(rows, t), sublane(inv, t)
            for u in range(t):
                x = x - low[t][u] * x_rows[u]
                v = v - low[t][u] * v_rows[u]
            x_rows[t] = x * rs[t]
            v_rows[t] = v * rs[t]
        packed = pack(v_rows)
        w_ref[o : o + 8, :] = packed
        for po in [o + 8 * m for m in range(1, AHEAD + 1) if q + m < 16]:
            d_rows, w_rows = d_ref[po : po + 8, :], w_ref[po : po + 8, :]
            coef = [None] * 8
            for t in range(8):
                c = lane(d_rows, o + t)
                for u in range(t):
                    c = c - coef[u] * low[t][u]
                coef[t] = c * rs[t]
            for t in range(8):
                d_rows = d_rows - coef[t] * x_rows[t]
                w_rows = w_rows - coef[t] * v_rows[t]
            d_ref[po : po + 8, :] = d_rows
            w_ref[po : po + 8, :] = w_rows
        if q < 15 - AHEAD:
            both = jnp.concatenate([pack(x_rows), packed], axis=1)
            high = both.astype(BF16).astype(F32)
            rest = both - high
            left = jnp.concatenate([high[:, :TILE], high[:, :TILE], rest[:, :TILE]], axis=0)
            right = jnp.concatenate([high, rest, high], axis=0)
            prod = lax.dot_general(
                left.astype(BF16), right.astype(BF16), (((0,), (0,)), ((), ())), preferred_element_type=F32
            )
            po = o + 8 * (AHEAD + 1)
            d_ref[po:, :] = d_ref[po:, :] - prod[po:, :TILE]
            w_ref[po:, :] = w_ref[po:, :] - prod[po:, TILE:]


def places():
    return lax.axis_index("leaf"), lax.axis_index("front")


def block(i):
    return pl.ds(pl.multiple_of(i * TILE, TILE), TILE)


def vspec(shape):
    return pl.BlockSpec(shape, lambda i: (0,) * len(shape))


def tiles_shape(n):
    return (n, TILE, TILE)


def call(kernel, name, us, ins, in_specs, outs, scratch):
    return pl.pallas_call(
        kernel,
        grid=(1,),
        in_specs=in_specs,
        out_specs=[vspec(s) for s, _ in outs],
        out_shape=[jax.ShapeDtypeStruct(s, t) for s, t in outs],
        scratch_shapes=scratch,
        compiler_params=params(),
        cost_estimate=cost(us),
        name=name,
    )(*ins)


def scatter(dst_ref, maps_ref, child, get_tile, rows, row_lo):
    for i in rows:
        mi = maps_ref[child, i] - row_lo

        @pl.when((mi >= 0) & (mi < 4))
        def _(i=i, mi=mi):
            for j in range(i + 1):
                dst_ref[block(mi), block(maps_ref[child, j])] += get_tile(i, j)


def tri(i, j):
    return i * (i + 1) // 2 + j


def pivot_head_kernel(level, maps_ref, *refs):
    pieces = refs[:8]
    tiles = refs[8 : len(refs) - 7]
    l_ref, t_ref, fs_ref, own_ref, f, d, w = refs[len(refs) - 7 :]
    leaf, y = places()
    core = leaf & 1
    n = SEP // (4 * 2**level)

    def put(ref, start, who, y_rel):
        pos = (who & (2**level - 1)) * 4 + ((y + y_rel) & 3)
        f[pl.ds(pl.multiple_of(pos * n, n), n), :] = ref[start : start + n, :]

    for i, rel in enumerate((0, 3, 1, 2)):
        for core_rel in range(2):
            ref = pieces[4 * core_rel + i]
            who = leaf ^ core_rel
            if level == 1:
                put(ref, 0, who, rel)
                continue
            for z1 in range(2):
                base = 64 * z1
                if level == 2:
                    put(ref, base, who ^ (z1 << 1), rel)
                else:
                    for z2 in range(2):
                        put(ref, base + 32 + 16 * z2, who ^ (z1 << 1) ^ (z2 << 2), rel)

    own = leaf >> (level - 1)
    sib = own ^ 1
    rows = range(4)
    if level == 1:
        for child, ref in ((own, tiles[0]), (sib, tiles[1])):
            scatter(f, maps_ref, child, lambda i, j, ref=ref: ref[tile_at(i), tile_at(j)], rows, 0)
    else:
        for c in range(2):

            @pl.when(core == c)
            def _(c=c):
                if level == 2:
                    for child, ref in ((own, tiles[c]), (sib, tiles[2 + c])):
                        scatter(f, maps_ref, child, lambda i, j, ref=ref: ref[tri(i, j)], rows, 0)
                else:
                    pair = (tiles[1 + c], tiles[2 - c])
                    scatter(f, maps_ref, own, lambda i, j: tiles[0][tri(i, j)], rows, 0)
                    scatter(f, maps_ref, sib, lambda i, j: pair[tri(i, j) // 5][tri(i, j) % 5], rows, 0)

    factor_pair(f, l_ref, t_ref, d, w, SEP)
    fs_ref[...] = f[HALF:, HALF:]
    pos = (leaf & (2**level - 1)) * 4 + y
    own_ref[...] = l_ref[pl.ds(pl.multiple_of(pos * n, n), n), :]


def tile_at(i):
    return slice(i * TILE, (i + 1) * TILE)


def factor_pair(f, l_ref, t_ref, d, w, order):
    ri = lax.broadcasted_iota(jnp.int32, (TILE, TILE), 0)
    ci = lax.broadcasted_iota(jnp.int32, (TILE, TILE), 1)
    for b in range(2):
        o = b * TILE
        d[...] = f[o : o + TILE, o : o + TILE]
        factor_tile(d, w)
        t_ref[b] = w[...]
        panel = dot_rows(f[o:order, o : o + TILE], w[...])
        if b:
            l_ref[:TILE, o : o + TILE] = jnp.zeros((TILE, TILE), F32)
        l_ref[o : o + TILE, o : o + TILE] = jnp.where(ri >= ci, panel[:TILE], 0.0)
        if o + TILE == order:
            continue
        below = panel[TILE:]
        l_ref[o + TILE :, o : o + TILE] = below
        high, low = split(below)
        for c in range(b + 1, order // TILE):
            k = (c - b - 1) * TILE
            at = slice(c * TILE, order)
            prod = dot_split((high[k:], low[k:]), (high[k : k + TILE], low[k : k + TILE]))
            f[at, tile_at(c)] = f[at, tile_at(c)] - prod


def pivot_tail_kernel(level, fs_ref, head_ref, l_ref, t_ref, own_ref, f, d, w):
    leaf, y = places()
    n = SEP // (4 * 2**level)
    f[...] = fs_ref[...]
    factor_pair(f, l_ref, t_ref, d, w, HALF)
    pos = ((leaf & (2**level - 1)) * 4 + y) * n
    own_ref[:, :HALF] = head_ref[...]

    @pl.when(pos < HALF)
    def _():
        own_ref[:, HALF:] = jnp.zeros((n, HALF), F32)

    @pl.when(pos >= HALF)
    def _():
        own_ref[:, HALF:] = l_ref[pl.ds(pl.multiple_of(pos - HALF, n), n), :]


def pivot_head(level, maps, pieces, tiles, tile_shapes):
    n = SEP // (4 * 2**level)
    size = 64 if level == 1 else 128
    return call(
        functools.partial(pivot_head_kernel, level), "pivot_head%d" % level, 11,
        [maps, *pieces, *tiles],
        [SMEM] + [vspec((size, SEP))] * 8 + [vspec(s) for s in tile_shapes],
        [((SEP, HALF), F32), (tiles_shape(2), F32), ((HALF, HALF), F32), ((n, HALF), F32)],
        [VM((SEP, SEP), F32), VM((TILE, TILE), F32), VM((TILE, TILE), F32)],
    )


def pivot_tail(level, fs, head):
    n = SEP // (4 * 2**level)
    return call(
        functools.partial(pivot_tail_kernel, level), "pivot_tail%d" % level, 9,
        [fs, head], [vspec((HALF, HALF)), vspec((n, HALF))],
        [((HALF, HALF), F32), (tiles_shape(2), F32), ((n, SEP), F32)],
        [VM((HALF, HALF), F32), VM((TILE, TILE), F32), VM((TILE, TILE), F32)],
    )


FACTOR = [vspec((SEP, HALF)), vspec(tiles_shape(2)), vspec((HALF, HALF)), vspec(tiles_shape(2))]


def solve_rows(get, factor, out_ref):
    la, ta, lb, tb = factor
    high, low = [], []
    for b in range(4):
        cols = get(b)
        for c in range(b):
            ref, rr, cc = (la, b, c) if c < 2 else (lb, b - 2, c - 2)
            cols = cols - dot_split((high[c], low[c]), split(ref[tile_at(rr), tile_at(cc)]))
        part = dot_rows(cols, (ta if b < 2 else tb)[b % 2])
        out_ref[:, tile_at(b)] = part
        ph, plo = split(part)
        high.append(ph)
        low.append(plo)
    return jnp.concatenate(high, axis=1), jnp.concatenate(low, axis=1)


def emit_lower(done, get, u_ref):
    for i in range(4):
        wide = (i + 1) * TILE
        prod = dot_split((done[0][tile_at(i)], done[1][tile_at(i)]), (done[0][:wide], done[1][:wide]))
        for j in range(i + 1):
            u_ref[tri(i, j)] = get(i, j) - prod[:, tile_at(j)]


def spread_kernel(maps_ref, own_ref, sib11_ref, sibr_ref, s21, s22, dst):
    leaf, _ = places()
    row_lo = 4 + 4 * (leaf & 1)
    dst[...] = jnp.zeros_like(dst)
    scatter(dst, maps_ref, leaf, lambda i, j: own_ref[tile_at(i), tile_at(j)], range(8), row_lo)
    get = lambda i, j: sib11_ref[tile_at(i), tile_at(j)] if i < 4 else sibr_ref[tile_at(i - 4), tile_at(j)]
    scatter(dst, maps_ref, leaf ^ 1, get, range(8), row_lo)
    s21[...] = dst[:, :SEP]
    s22[...] = dst[:, SEP:]


def spread(maps, own, sib11, sibr):
    return call(
        spread_kernel, "spread", 7, [maps, own, sib11, sibr],
        [SMEM, vspec((UPD, UPD)), vspec((SEP, SEP)), vspec((SEP, UPD))],
        [((SEP, SEP), F32), ((SEP, UPD), F32)], [VM((SEP, SEP + UPD), F32)],
    )


def solve_kernel_1(la, ta, lb, tb, s21, e0, e1, e2, e3, l21_ref, below_ref, x):
    _, y = places()
    x[...] = s21[...]
    for ref, rel in ((e0, 0), (e1, 3), (e2, 1), (e3, 2)):
        x[block((y + rel) & 3), :] += ref[...]
    solve_rows(lambda b: x[:, tile_at(b)], (la, ta, lb, tb), l21_ref)
    below_ref[...] = l21_ref[block(y), :]


def solve_1(factor, s21, pieces):
    return call(
        solve_kernel_1, "solve1", 4, [*factor, s21, *pieces],
        FACTOR + [vspec((SEP, SEP))] + [vspec((TILE, SEP))] * 4,
        [((SEP, SEP), F32), ((TILE, SEP), F32)], [VM((SEP, SEP), F32)],
    )


def diag_kernel_1(l21_ref, s22, g_ref, u_ref, e, t, sem):
    leaf, _ = places()
    at = pl.ds(pl.multiple_of((leaf & 1) * SEP, SEP), SEP)
    first = pltpu.make_async_copy(g_ref.at[:, :, at], e, sem.at[0])
    second = pltpu.make_async_copy(s22.at[:, at], t, sem.at[1])
    first.start()
    second.start()
    done = split(l21_ref[...])
    first.wait()
    second.wait()
    emit_lower(done, lambda i, j: e[i, :, tile_at(j)] + t[tile_at(i), tile_at(j)], u_ref)


def diag_1(l21, s22, g1):
    return call(
        diag_kernel_1, "diag1", 4, [l21, s22, g1], [vspec((SEP, SEP)), ANY, ANY],
        [(tiles_shape(10), F32)],
        [VM((4, TILE, SEP), F32), VM((SEP, SEP), F32), pltpu.SemaphoreType.DMA((2,))],
    )[0]


def cross_kernel_1(l21_ref, other_ref, s22, g_ref, u_ref, e, t, sem):
    leaf, _ = places()
    at = pl.ds(0, SEP)
    first = pltpu.make_async_copy(g_ref.at[:, :, at], e, sem.at[0])
    second = pltpu.make_async_copy(s22.at[:, at], t, sem.at[1])
    first.start()
    second.start()
    first.wait()
    second.wait()

    @pl.when((leaf & 1) == 1)
    def _():
        top = split(other_ref[...])
        for i in range(4):
            prod = dot_split(split(l21_ref[tile_at(i), :]), top)
            for j in range(4):
                u_ref[4 * i + j] = (e[i, :, tile_at(j)] + t[tile_at(i), tile_at(j)]) - prod[:, tile_at(j)]


def cross_1(l21, other, s22, g1):
    return call(
        cross_kernel_1, "cross1", 5, [l21, other, s22, g1], [vspec((SEP, SEP)), vspec((SEP, SEP)), ANY, ANY],
        [(tiles_shape(16), F32)],
        [VM((4, TILE, SEP), F32), VM((SEP, SEP), F32), pltpu.SemaphoreType.DMA((2,))],
    )[0]


def load_tiles(pairs, core, bufs, sem):
    for k, (pair, buf) in enumerate(zip(pairs, bufs)):
        for c in range(2):

            @pl.when(core == c)
            def _(pair=pair, buf=buf, c=c, k=k):
                pltpu.make_async_copy(pair[c], buf, sem.at[k]).start()

    return [pltpu.make_async_copy(pair[0], buf, sem.at[k]) for k, (pair, buf) in enumerate(zip(pairs, bufs))]


def load_rows_2(which, g_own, g_sw, e, sem, base):
    leaf, _ = places()
    core = leaf & 1
    z_rel = ((leaf >> 1) & 1) ^ which
    copies = []
    for y in range(4):
        for part in range(2):
            for src, who in ((g_own, core), (g_sw, 1 - core)):
                row = pl.multiple_of(who * 256 + y * 64, 64)
                dst = e.at[pl.ds(row, 64), part * SEP : (part + 1) * SEP]
                copies.append(pltpu.make_async_copy(src.at[y, z_rel, part], dst, sem.at[base + len(copies)]))
    for c in copies:
        c.start()
    return copies


def tile_getter(t11, tba, tbb):
    def get(i, j):
        if i < 4:
            return t11[tri(i, j)]
        if j < 4:
            return tba[4 * (i - 4) + j]
        return tbb[tri(i - 4, j - 4)]

    return get


def upper_kernel_2(maps_ref, la, ta, lb, tb, *refs):
    held, (g_own, g_sw, l21_ref, u_ref, half_ref, e, sem), bufs = refs[:12], refs[12:19], refs[19:]
    leaf, _ = places()
    core = leaf & 1
    copies = load_rows_2(0, g_own, g_sw, e, sem, 6)
    copies += load_tiles([(held[2 * k], held[2 * k + 1]) for k in range(6)], core, bufs, sem)
    for c in copies:
        c.wait()
    own = leaf >> 1
    scatter(e, maps_ref, own, tile_getter(*bufs[:3]), range(7), 4)
    scatter(e, maps_ref, own ^ 1, tile_getter(*bufs[3:]), range(7), 4)
    done = solve_rows(lambda b: e[:, tile_at(b)], (la, ta, lb, tb), l21_ref)
    emit_lower(done, lambda i, j: e[tile_at(i), tile_at(4 + j)], u_ref)
    half_ref[...] = u_ref[pl.ds(core * 5, 5)]


def upper_2(maps, factor, held, g_own, g_sw):
    return call(
        upper_kernel_2, "upper2", 9, [maps, *factor, *held, g_own, g_sw],
        [SMEM] + FACTOR + [ANY] * 14,
        [((SEP, SEP), F32), (tiles_shape(10), F32), (tiles_shape(5), F32)],
        [VM((SEP, UPD), F32), pltpu.SemaphoreType.DMA((22,))] + [VM(tiles_shape(n), F32) for n in (10, 16, 10) * 2],
    )


def lower_kernel_2(maps_ref, maps3_ref, la, ta, lb, tb, l21a, u10, *refs):
    held, (g_own, g_sw, mine_ref, send_ref, below_ref, e, l21b, u21, sem), bufs = refs[:8], refs[8:17], refs[17:]
    leaf, y = places()
    core = leaf & 1
    e[:, UPD:] = jnp.zeros((SEP, SEP), F32)
    copies = load_rows_2(1, g_own, g_sw, e, sem, 4)
    copies += load_tiles([(held[2 * k], held[2 * k + 1]) for k in range(4)], core, bufs, sem)
    for c in copies:
        c.wait()
    own = leaf >> 1
    scatter(e, maps_ref, own, tile_getter(None, *bufs[:2]), range(4, 8), 8)
    scatter(e, maps_ref, own ^ 1, tile_getter(None, *bufs[2:]), range(4, 8), 8)
    done = solve_rows(lambda b: e[:, tile_at(b)], (la, ta, lb, tb), l21b)
    u21[...] = e[:, SEP:UPD] - dot_split(done, split(l21a[...]))
    child = leaf >> 2
    stripe = pl.ds(pl.multiple_of(y * 32, 32), 32)
    for out_ref, who in ((mine_ref, leaf), (send_ref, leaf ^ 4)):
        out_ref[...] = jnp.zeros_like(out_ref)
        want = 4 + (who & 7)
        for j in range(1, 8):

            @pl.when(maps3_ref[child, j] == want)
            def _(j=j, out_ref=out_ref):
                for c in range(min(j, 4)):
                    mj = maps3_ref[child, c]

                    @pl.when(mj < 4)
                    def _(c=c, mj=mj):
                        if j < 4:
                            piece = u10[tri(j, c), stripe, :]
                        else:
                            row = pl.multiple_of((j - 4) * TILE + y * 32, 32)
                            piece = u21[pl.ds(row, 32), tile_at(c)]
                        out_ref[:, block(mj)] = piece

    pos = ((leaf & 3) * 4 + y) * 64

    @pl.when(pos < SEP)
    def _():
        below_ref[...] = l21a[pl.ds(pl.multiple_of(pos, 64), 64), :]

    @pl.when(pos >= SEP)
    def _():
        below_ref[...] = l21b[pl.ds(pl.multiple_of(pos - SEP, 64), 64), :]


def lower_2(maps, maps3, factor, l21a, u10, held, g_own, g_sw):
    return call(
        lower_kernel_2, "lower2", 9, [maps, maps3, *factor, l21a, u10, *held, g_own, g_sw],
        [SMEM] * 2 + FACTOR + [vspec((SEP, SEP)), vspec(tiles_shape(10))] + [ANY] * 10,
        [((32, SEP), F32), ((32, SEP), F32), ((64, SEP), F32)],
        [VM((SEP, SEP + UPD), F32), VM((SEP, SEP), F32), VM((SEP, SEP), F32), pltpu.SemaphoreType.DMA((20,))]
        + [VM(tiles_shape(n), F32) for n in (16, 10) * 2],
    )


def last_kernel(la, ta, lb, tb, e_ref, mine_ref, got_ref, out_ref):
    x = e_ref[...] + mine_ref[...] + got_ref[...]
    solve_rows(lambda b: x[:, tile_at(b)], (la, ta, lb, tb), out_ref)


def last(factor, rem3, mine, got):
    return call(
        last_kernel, "last", 3, [*factor, rem3, mine, got], FACTOR + [vspec((32, SEP))] * 3, [((32, SEP), F32)], []
    )[0]


def swap(x, bit, cores=(0, 1)):
    n = lax.axis_size("leaf")
    return lax.ppermute(x, "leaf", [(i, i ^ (1 << bit)) for i in range(n) if i % 2 in cores])


def shift(x, d):
    n = lax.axis_size("front")
    return lax.ppermute(x, "front", [(i, (i + d) % n) for i in range(n)])


def around(x):
    return [x, shift(x, 1), shift(x, -1), shift(x, 2)]


def after(x, *deps):
    return lax.optimization_barrier((x,) + deps)[0]


def body(leaf_update, sep1, rem1, sep2, rem2, sep3, rem3, map1, map2, map3):
    e11 = around(sep1[:, :SEP])
    u_sib11 = swap(leaf_update[:SEP, :SEP], 0)
    u_sibr = swap(leaf_update[SEP:, :], 0)
    s3z = swap(sep3[:, :SEP], 2)
    e21 = around(after(rem1[:, :SEP], u_sib11))
    g1 = lax.all_gather(rem1[:, SEP:], "front", axis=0, tiled=False)
    s21, s22 = spread(map1, leaf_update, u_sib11, u_sibr)
    s3 = jnp.concatenate([sep2[:, :SEP], sep3[:, :SEP], s3z], axis=0)
    s3 = jnp.concatenate([s3, swap(s3, 1)], axis=0)
    r2 = jnp.stack([rem2[:, :SEP], rem2[:, SEP:UPD]])
    r2 = jnp.stack([r2, swap(r2, 1)])
    pieces = e11 + [swap(x, 0) for x in e11]
    pieces[0] = after(pieces[0], s21, s3, r2)
    la, ta, fs, head = pivot_head(1, map1, pieces, [leaf_update, u_sib11], [(SEP, SEP)] * 2)
    g2 = lax.all_gather(after(r2, ta), "front", axis=0, tiled=False)
    lb, tb, out_p1 = pivot_tail(1, fs, head)
    l21, out_b1 = solve_1((la, ta, lb, tb), s21, e21[:1] + [after(x, tb) for x in e21[1:]])
    other = swap(l21, 0)
    uhh = diag_1(l21, s22, after(g1, l21))
    z11 = swap(uhh, 1, (0,))
    uhh_sw = swap(uhh, 0)
    e2 = around(after(s3, uhh))
    uba = cross_1(l21, after(other, uhh), s22, g1)
    z11_sw = swap(z11, 0)
    e2 = e2 + [swap(x, 0) for x in e2]
    uba_sw = swap(after(uba, z11), 0)
    zbb = swap(after(uhh, z11), 1, (1,))
    zba = swap(after(uba, z11), 1, (1,))
    la, ta, fs, head = pivot_head(2, map2, e2, [uhh, uhh_sw, z11, z11_sw], [tiles_shape(10)] * 4)
    lb, tb, out_p2 = pivot_tail(2, fs, head)
    zbb, zba, g2 = lax.optimization_barrier((zbb, zba, g2, tb))[:3]
    factor = (la, ta, lb, tb)
    g2_sw = swap(g2, 0)
    zbb_sw = swap(zbb, 0)
    zba_sw = swap(zba, 0)
    held = [uhh, uhh_sw, uba_sw, uba, uhh_sw, uhh, z11, z11_sw, zba_sw, zba, zbb_sw, zbb]
    l21a, v10, half = upper_2(map2, factor, held, g2, g2_sw)
    half_z = swap(half, 2)
    mine, send, out_b2 = lower_2(map2, map3, factor, l21a, v10, held[2:6] + held[8:], g2, g2_sw)
    half_z = after(half_z, mine)
    half_sw = swap(half_z, 0)
    got = swap(send, 2)
    la, ta, fs, head = pivot_head(3, map3, e2, [v10, half_z, half_sw], [tiles_shape(n) for n in (10, 5, 5)])
    lb, tb, out_p3 = pivot_tail(3, fs, head)
    out_b3 = last((la, ta, lb, tb), rem3, mine, after(got, tb))
    return out_p1, out_b1, out_p2, out_b2, out_p3, out_b3


def solution(mesh):
    both = P(("leaf", "front"), None)
    in_specs = (P("leaf", None),) + (both,) * 6 + (P(), P(), P())
    return jax.shard_map(body, mesh=mesh, in_specs=in_specs, out_specs=(both,) * 6, check_vma=False)
```

```python
import functools
import jax
import jax.numpy as jnp
from jax import lax
from jax.experimental import pallas as pl
from jax.experimental.pallas import tpu as pltpu
from jax.sharding import PartitionSpec as P

TILE = 128
SEP = 512
UPD = 1024
F32 = jnp.float32
BF16 = jnp.bfloat16
AHEAD = 3
HALF = SEP // 2
ANY = pl.BlockSpec(memory_space=pl.ANY)
SMEM = pl.BlockSpec(memory_space=pltpu.SMEM)
VM = pltpu.VMEM
ROWS = (((1,), (1,)), ((), ()))


def params():
    return pltpu.CompilerParams(vmem_limit_bytes=56 << 20)


def cost(us):
    return pl.CostEstimate(flops=int(us * 1e6), bytes_accessed=int(us * 3e3), transcendentals=0)


def split(a):
    high = a.astype(BF16)
    return high, (a - high.astype(F32)).astype(BF16)


def dot_split(a, b):
    ah, al = a
    bh, bl = b
    mul = lambda x, y: lax.dot_general(x, y, ROWS, preferred_element_type=F32)
    return mul(ah, bh) + (mul(ah, bl) + mul(al, bh))


def dot_rows(a, b):
    return dot_split(split(a), split(b))


def lane(x, c):
    return jnp.broadcast_to(x[:, c : c + 1], (8, TILE))


def sublane(x, r):
    return jnp.broadcast_to(x[r : r + 1, :], (8, TILE))


def factor_tile(d_ref, w_ref):
    rows8 = lax.broadcasted_iota(jnp.int32, (8, TILE), 0)
    ri = lax.broadcasted_iota(jnp.int32, (TILE, TILE), 0)
    ci = lax.broadcasted_iota(jnp.int32, (TILE, TILE), 1)
    w_ref[...] = jnp.where(ri == ci, 1.0, 0.0).astype(F32)

    def pack(parts):
        out = parts[0]
        for t in range(1, 8):
            out = jnp.where(rows8 == t, parts[t], out)
        return out

    for q in range(16):
        o = 8 * q
        rows, inv = d_ref[o : o + 8, :], w_ref[o : o + 8, :]
        cols = [lane(rows, o + t) for t in range(8)]
        a = [[None] * 8 for _ in range(8)]
        for t in range(8):
            for s in range(t, 8):
                a[s][t] = sublane(cols[t], s)
        rs = [None] * 8
        low = [[None] * 8 for _ in range(8)]
        x_rows = [None] * 8
        v_rows = [None] * 8
        for t in range(0, 8, 2):
            aa, bb, cc = a[t][t], a[t + 1][t], a[t + 1][t + 1]
            rs[t] = lax.rsqrt(aa)
            rs[t + 1] = lax.rsqrt(aa * cc - bb * bb) * (aa * rs[t])
            low[t + 1][t] = bb * rs[t]
            for s in range(t + 2, 8):
                low[s][t] = a[s][t] * rs[t]
                low[s][t + 1] = (a[s][t + 1] - low[s][t] * low[t + 1][t]) * rs[t + 1]
            for s in range(t + 2, 8):
                for u in range(t + 2, s + 1):
                    a[s][u] = (a[s][u] - low[s][t] * low[u][t]) - low[s][t + 1] * low[u][t + 1]
        for t in range(8):
            x, v = sublane(rows, t), sublane(inv, t)
            for u in range(t):
                x = x - low[t][u] * x_rows[u]
                v = v - low[t][u] * v_rows[u]
            x_rows[t] = x * rs[t]
            v_rows[t] = v * rs[t]
        packed = pack(v_rows)
        w_ref[o : o + 8, :] = packed
        for po in [o + 8 * m for m in range(1, AHEAD + 1) if q + m < 16]:
            d_rows, w_rows = d_ref[po : po + 8, :], w_ref[po : po + 8, :]
            coef = [None] * 8
            for t in range(8):
                c = lane(d_rows, o + t)
                for u in range(t):
                    c = c - coef[u] * low[t][u]
                coef[t] = c * rs[t]
            for t in range(8):
                d_rows = d_rows - coef[t] * x_rows[t]
                w_rows = w_rows - coef[t] * v_rows[t]
            d_ref[po : po + 8, :] = d_rows
            w_ref[po : po + 8, :] = w_rows
        if q < 15 - AHEAD:
            both = jnp.concatenate([pack(x_rows), packed], axis=1)
            high = both.astype(BF16).astype(F32)
            rest = both - high
            left = jnp.concatenate([high[:, :TILE], high[:, :TILE], rest[:, :TILE]], axis=0)
            right = jnp.concatenate([high, rest, high], axis=0)
            prod = lax.dot_general(
                left.astype(BF16), right.astype(BF16), (((0,), (0,)), ((), ())), preferred_element_type=F32
            )
            po = o + 8 * (AHEAD + 1)
            d_ref[po:, :] = d_ref[po:, :] - prod[po:, :TILE]
            w_ref[po:, :] = w_ref[po:, :] - prod[po:, TILE:]


def places():
    return lax.axis_index("leaf"), lax.axis_index("front")


def block(i):
    return pl.ds(pl.multiple_of(i * TILE, TILE), TILE)


def vspec(shape):
    return pl.BlockSpec(shape, lambda i: (0,) * len(shape))


def tiles_shape(n):
    return (n, TILE, TILE)


def call(kernel, name, us, ins, in_specs, outs, scratch):
    return pl.pallas_call(
        kernel,
        grid=(1,),
        in_specs=in_specs,
        out_specs=[vspec(s) for s, _ in outs],
        out_shape=[jax.ShapeDtypeStruct(s, t) for s, t in outs],
        scratch_shapes=scratch,
        compiler_params=params(),
        cost_estimate=cost(us),
        name=name,
    )(*ins)


def scatter(dst_ref, maps_ref, child, get_tile, rows, row_lo):
    for i in rows:
        mi = maps_ref[child, i] - row_lo

        @pl.when((mi >= 0) & (mi < 4))
        def _(i=i, mi=mi):
            for j in range(i + 1):
                dst_ref[block(mi), block(maps_ref[child, j])] += get_tile(i, j)


def tri(i, j):
    return i * (i + 1) // 2 + j


def pivot_head_kernel(level, maps_ref, *refs):
    n_pieces = (2, 4, 8)[level - 1]
    pieces, tiles = refs[:n_pieces], refs[n_pieces : len(refs) - 7]
    l_ref, t_ref, fs_ref, own_ref, f, d, w = refs[len(refs) - 7 :]
    leaf, y = places()
    core = leaf & 1
    n = SEP // (4 * 2**level)

    def put(ref, start, who, y_rel):
        pos = (who & (2**level - 1)) * 4 + ((y + y_rel) & 3)
        f[pl.ds(pl.multiple_of(pos * n, n), n), :] = ref[start : start + n, :]

    for i, rel in enumerate((0, 3, 1, 2)):
        for core_rel in range(2):
            who = leaf ^ core_rel
            if level == 1:
                put(pieces[core_rel], 64 * i, who, rel)
                continue
            for z1 in range(2):
                ref, at_z1 = pieces[2 * core_rel + z1], who ^ (z1 << 1)
                if level == 2:
                    put(ref, 48 * i, at_z1, rel)
                else:
                    put(ref, 48 * i + 32, at_z1, rel)
                    put(pieces[4 + 2 * core_rel + z1], 16 * i, at_z1 ^ 4, rel)

    own = leaf >> (level - 1)
    sib = own ^ 1
    rows = range(4)
    if level == 1:
        for child, ref in ((own, tiles[0]), (sib, tiles[1])):
            scatter(f, maps_ref, child, lambda i, j, ref=ref: ref[tile_at(i), tile_at(j)], rows, 0)
    else:
        for c in range(2):

            @pl.when(core == c)
            def _(c=c):
                if level == 2:
                    for child, ref in ((own, tiles[c]), (sib, tiles[2 + c])):
                        scatter(f, maps_ref, child, lambda i, j, ref=ref: ref[tri(i, j)], rows, 0)
                else:
                    pair = (tiles[1 + c], tiles[2 - c])
                    scatter(f, maps_ref, own, lambda i, j: tiles[0][tri(i, j)], rows, 0)
                    scatter(f, maps_ref, sib, lambda i, j: pair[tri(i, j) // 5][tri(i, j) % 5], rows, 0)

    factor_pair(f, l_ref, t_ref, d, w, SEP)
    fs_ref[...] = f[HALF:, HALF:]
    pos = (leaf & (2**level - 1)) * 4 + y
    own_ref[...] = l_ref[pl.ds(pl.multiple_of(pos * n, n), n), :]


def tile_at(i):
    return slice(i * TILE, (i + 1) * TILE)


def factor_pair(f, l_ref, t_ref, d, w, order):
    ri = lax.broadcasted_iota(jnp.int32, (TILE, TILE), 0)
    ci = lax.broadcasted_iota(jnp.int32, (TILE, TILE), 1)
    for b in range(2):
        o = b * TILE
        d[...] = f[o : o + TILE, o : o + TILE]
        factor_tile(d, w)
        t_ref[b] = w[...]
        panel = dot_rows(f[o:order, o : o + TILE], w[...])
        if b:
            l_ref[:TILE, o : o + TILE] = jnp.zeros((TILE, TILE), F32)
        l_ref[o : o + TILE, o : o + TILE] = jnp.where(ri >= ci, panel[:TILE], 0.0)
        if o + TILE == order:
            continue
        below = panel[TILE:]
        l_ref[o + TILE :, o : o + TILE] = below
        high, low = split(below)
        for c in range(b + 1, order // TILE):
            k = (c - b - 1) * TILE
            at = slice(c * TILE, order)
            prod = dot_split((high[k:], low[k:]), (high[k : k + TILE], low[k : k + TILE]))
            f[at, tile_at(c)] = f[at, tile_at(c)] - prod


def pivot_tail_kernel(level, fs_ref, head_ref, l_ref, t_ref, own_ref, f, d, w):
    leaf, y = places()
    n = SEP // (4 * 2**level)
    f[...] = fs_ref[...]
    factor_pair(f, l_ref, t_ref, d, w, HALF)
    pos = ((leaf & (2**level - 1)) * 4 + y) * n
    own_ref[:, :HALF] = head_ref[...]

    @pl.when(pos < HALF)
    def _():
        own_ref[:, HALF:] = jnp.zeros((n, HALF), F32)

    @pl.when(pos >= HALF)
    def _():
        own_ref[:, HALF:] = l_ref[pl.ds(pl.multiple_of(pos - HALF, n), n), :]


def pivot_head(level, maps, pieces, tiles, tile_shapes):
    n = SEP // (4 * 2**level)
    return call(
        functools.partial(pivot_head_kernel, level), "pivot_head%d" % level, 11,
        [maps, *pieces, *tiles],
        [SMEM] + [vspec(p.shape) for p in pieces] + [vspec(s) for s in tile_shapes],
        [((SEP, HALF), F32), (tiles_shape(2), F32), ((HALF, HALF), F32), ((n, HALF), F32)],
        [VM((SEP, SEP), F32), VM((TILE, TILE), F32), VM((TILE, TILE), F32)],
    )


def pivot_tail(level, fs, head):
    n = SEP // (4 * 2**level)
    return call(
        functools.partial(pivot_tail_kernel, level), "pivot_tail%d" % level, 9,
        [fs, head], [vspec((HALF, HALF)), vspec((n, HALF))],
        [((HALF, HALF), F32), (tiles_shape(2), F32), ((n, SEP), F32)],
        [VM((HALF, HALF), F32), VM((TILE, TILE), F32), VM((TILE, TILE), F32)],
    )


FACTOR = [vspec((SEP, HALF)), vspec(tiles_shape(2)), vspec((HALF, HALF)), vspec(tiles_shape(2))]


def solve_rows(get, factor, out_ref):
    la, ta, lb, tb = factor
    high, low = [], []
    for b in range(4):
        cols = get(b)
        for c in range(b):
            ref, rr, cc = (la, b, c) if c < 2 else (lb, b - 2, c - 2)
            cols = cols - dot_split((high[c], low[c]), split(ref[tile_at(rr), tile_at(cc)]))
        part = dot_rows(cols, (ta if b < 2 else tb)[b % 2])
        out_ref[:, tile_at(b)] = part
        ph, plo = split(part)
        high.append(ph)
        low.append(plo)
    return jnp.concatenate(high, axis=1), jnp.concatenate(low, axis=1)


def emit_lower(done, get, u_ref):
    for i in range(4):
        wide = (i + 1) * TILE
        prod = dot_split((done[0][tile_at(i)], done[1][tile_at(i)]), (done[0][:wide], done[1][:wide]))
        for j in range(i + 1):
            u_ref[tri(i, j)] = get(i, j) - prod[:, tile_at(j)]


def spread_kernel(maps_ref, own_ref, sib_ref, s21, s22, dst):
    leaf, _ = places()
    row_lo = 4 + 4 * (leaf & 1)
    dst[...] = jnp.zeros_like(dst)
    for child, ref in ((leaf, own_ref), (leaf ^ 1, sib_ref)):
        scatter(dst, maps_ref, child, lambda i, j, ref=ref: ref[tile_at(i), tile_at(j)], range(8), row_lo)
    s21[...] = dst[:, :SEP]
    s22[...] = dst[:, SEP:]


def spread(maps, own, sib):
    return call(
        spread_kernel, "spread", 7, [maps, own, sib], [SMEM, vspec((UPD, UPD)), vspec((UPD, UPD))],
        [((SEP, SEP), F32), ((SEP, UPD), F32)], [VM((SEP, SEP + UPD), F32)],
    )


def solve_kernel_1(la, ta, lb, tb, s21, e0, e1, e2, e3, l21_ref, below_ref, x):
    _, y = places()
    x[...] = s21[...]
    for ref, rel in ((e0, 0), (e1, 3), (e2, 1), (e3, 2)):
        x[block((y + rel) & 3), :] += ref[...]
    solve_rows(lambda b: x[:, tile_at(b)], (la, ta, lb, tb), l21_ref)
    below_ref[...] = l21_ref[block(y), :]


def solve_1(factor, s21, pieces):
    return call(
        solve_kernel_1, "solve1", 4, [*factor, s21, *pieces],
        FACTOR + [vspec((SEP, SEP))] + [vspec((TILE, SEP))] * 4,
        [((SEP, SEP), F32), ((TILE, SEP), F32)], [VM((SEP, SEP), F32)],
    )


def diag_kernel_1(l21_ref, s22, g_ref, u_ref, e, t, sem):
    leaf, _ = places()
    at = pl.ds(pl.multiple_of((leaf & 1) * SEP, SEP), SEP)
    first = pltpu.make_async_copy(g_ref.at[:, :, at], e, sem.at[0])
    second = pltpu.make_async_copy(s22.at[:, at], t, sem.at[1])
    first.start()
    second.start()
    done = split(l21_ref[...])
    first.wait()
    second.wait()
    emit_lower(done, lambda i, j: e[i, :, tile_at(j)] + t[tile_at(i), tile_at(j)], u_ref)


def diag_1(l21, s22, g1):
    return call(
        diag_kernel_1, "diag1", 4, [l21, s22, g1], [vspec((SEP, SEP)), ANY, ANY],
        [(tiles_shape(10), F32)],
        [VM((4, TILE, SEP), F32), VM((SEP, SEP), F32), pltpu.SemaphoreType.DMA((2,))],
    )[0]


def cross_kernel_1(l21_ref, other_ref, s22, g_ref, u_ref, e, t, sem):
    leaf, _ = places()
    at = pl.ds(0, SEP)
    first = pltpu.make_async_copy(g_ref.at[:, :, at], e, sem.at[0])
    second = pltpu.make_async_copy(s22.at[:, at], t, sem.at[1])
    first.start()
    second.start()
    first.wait()
    second.wait()

    @pl.when((leaf & 1) == 1)
    def _():
        top = split(other_ref[...])
        for i in range(4):
            prod = dot_split(split(l21_ref[tile_at(i), :]), top)
            for j in range(4):
                u_ref[4 * i + j] = (e[i, :, tile_at(j)] + t[tile_at(i), tile_at(j)]) - prod[:, tile_at(j)]


def cross_1(l21, other, s22, g1):
    return call(
        cross_kernel_1, "cross1", 5, [l21, other, s22, g1], [vspec((SEP, SEP)), vspec((SEP, SEP)), ANY, ANY],
        [(tiles_shape(16), F32)],
        [VM((4, TILE, SEP), F32), VM((SEP, SEP), F32), pltpu.SemaphoreType.DMA((2,))],
    )[0]


def load_tiles(pairs, core, bufs, sem):
    for k, (pair, buf) in enumerate(zip(pairs, bufs)):
        for c in range(2):

            @pl.when(core == c)
            def _(pair=pair, buf=buf, c=c, k=k):
                pltpu.make_async_copy(pair[c], buf, sem.at[k]).start()

    return [pltpu.make_async_copy(pair[0], buf, sem.at[k]) for k, (pair, buf) in enumerate(zip(pairs, bufs))]


def load_rows_2(which, g_own, g_sw, e, sem, base):
    leaf, _ = places()
    core = leaf & 1
    z_rel = ((leaf >> 1) & 1) ^ which
    copies = []
    for y in range(4):
        for part in range(2):
            for src, who in ((g_own, core), (g_sw, 1 - core)):
                row = pl.multiple_of(who * 256 + y * 64, 64)
                dst = e.at[pl.ds(row, 64), part * SEP : (part + 1) * SEP]
                copies.append(pltpu.make_async_copy(src.at[y, z_rel, part * 64 : (part + 1) * 64], dst, sem.at[base + len(copies)]))
    for c in copies:
        c.start()
    return copies


def tile_getter(t11, tba, tbb):
    def get(i, j):
        if i < 4:
            return t11[tri(i, j)]
        if j < 4:
            return tba[4 * (i - 4) + j]
        return tbb[tri(i - 4, j - 4)]

    return get


def upper_kernel_2(maps_ref, la, ta, lb, tb, *refs):
    held, (g_own, g_sw, l21_ref, u_ref, half_ref, e, sem), bufs = refs[:12], refs[12:19], refs[19:]
    leaf, _ = places()
    core = leaf & 1
    copies = load_rows_2(0, g_own, g_sw, e, sem, 6)
    copies += load_tiles([(held[2 * k], held[2 * k + 1]) for k in range(6)], core, bufs, sem)
    for c in copies:
        c.wait()
    own = leaf >> 1
    scatter(e, maps_ref, own, tile_getter(*bufs[:3]), range(7), 4)
    scatter(e, maps_ref, own ^ 1, tile_getter(*bufs[3:]), range(7), 4)
    done = solve_rows(lambda b: e[:, tile_at(b)], (la, ta, lb, tb), l21_ref)
    emit_lower(done, lambda i, j: e[tile_at(i), tile_at(4 + j)], u_ref)
    half_ref[...] = u_ref[pl.ds(core * 5, 5)]


def upper_2(maps, factor, held, g_own, g_sw):
    return call(
        upper_kernel_2, "upper2", 9, [maps, *factor, *held, g_own, g_sw],
        [SMEM] + FACTOR + [ANY] * 14,
        [((SEP, SEP), F32), (tiles_shape(10), F32), (tiles_shape(5), F32)],
        [VM((SEP, UPD), F32), pltpu.SemaphoreType.DMA((22,))] + [VM(tiles_shape(n), F32) for n in (10, 16, 10) * 2],
    )


def lower_kernel_2(maps_ref, maps3_ref, la, ta, lb, tb, l21a, u10, *refs):
    held, (g_own, g_sw, mine_ref, send_ref, below_ref, e, l21b, u21, sem), bufs = refs[:8], refs[8:17], refs[17:]
    leaf, y = places()
    core = leaf & 1
    e[:, UPD:] = jnp.zeros((SEP, SEP), F32)
    copies = load_rows_2(1, g_own, g_sw, e, sem, 4)
    copies += load_tiles([(held[2 * k], held[2 * k + 1]) for k in range(4)], core, bufs, sem)
    for c in copies:
        c.wait()
    own = leaf >> 1
    scatter(e, maps_ref, own, tile_getter(None, *bufs[:2]), range(4, 8), 8)
    scatter(e, maps_ref, own ^ 1, tile_getter(None, *bufs[2:]), range(4, 8), 8)
    done = solve_rows(lambda b: e[:, tile_at(b)], (la, ta, lb, tb), l21b)
    u21[...] = e[:, SEP:UPD] - dot_split(done, split(l21a[...]))
    child = leaf >> 2
    stripe = pl.ds(pl.multiple_of(y * 32, 32), 32)
    for out_ref, who in ((mine_ref, leaf), (send_ref, leaf ^ 4)):
        out_ref[...] = jnp.zeros_like(out_ref)
        want = 4 + (who & 7)
        for j in range(1, 8):

            @pl.when(maps3_ref[child, j] == want)
            def _(j=j, out_ref=out_ref):
                for c in range(min(j, 4)):
                    mj = maps3_ref[child, c]

                    @pl.when(mj < 4)
                    def _(c=c, mj=mj):
                        if j < 4:
                            piece = u10[tri(j, c), stripe, :]
                        else:
                            row = pl.multiple_of((j - 4) * TILE + y * 32, 32)
                            piece = u21[pl.ds(row, 32), tile_at(c)]
                        out_ref[:, block(mj)] = piece

    pos = ((leaf & 3) * 4 + y) * 64

    @pl.when(pos < SEP)
    def _():
        below_ref[...] = l21a[pl.ds(pl.multiple_of(pos, 64), 64), :]

    @pl.when(pos >= SEP)
    def _():
        below_ref[...] = l21b[pl.ds(pl.multiple_of(pos - SEP, 64), 64), :]


def lower_2(maps, maps3, factor, l21a, u10, held, g_own, g_sw):
    return call(
        lower_kernel_2, "lower2", 9, [maps, maps3, *factor, l21a, u10, *held, g_own, g_sw],
        [SMEM] * 2 + FACTOR + [vspec((SEP, SEP)), vspec(tiles_shape(10))] + [ANY] * 10,
        [((32, SEP), F32), ((32, SEP), F32), ((64, SEP), F32)],
        [VM((SEP, SEP + UPD), F32), VM((SEP, SEP), F32), VM((SEP, SEP), F32), pltpu.SemaphoreType.DMA((20,))]
        + [VM(tiles_shape(n), F32) for n in (16, 10) * 2],
    )


def last_kernel(la, ta, lb, tb, e_ref, mine_ref, got_ref, out_ref):
    x = e_ref[...] + mine_ref[...] + got_ref[...]
    solve_rows(lambda b: x[:, tile_at(b)], (la, ta, lb, tb), out_ref)


def last(factor, rem3, mine, got):
    return call(
        last_kernel, "last", 3, [*factor, rem3, mine, got], FACTOR + [vspec((32, SEP))] * 3, [((32, SEP), F32)], []
    )[0]


def copy_kernel(plan, n_in, *refs):
    ins, outs, sem = refs[:n_in], refs[n_in:-1], refs[-1]
    copies = []
    for k, (src, src_at, dst, dst_at) in enumerate(plan):
        copies.append(pltpu.make_async_copy(ins[src].at[src_at], outs[dst].at[dst_at], sem.at[k]))
    for c in copies:
        c.start()
    for c in copies:
        c.wait()


def copies(name, plan, ins, shapes):
    return pl.pallas_call(
        functools.partial(copy_kernel, plan, len(ins)),
        in_specs=[ANY] * len(ins),
        out_specs=[ANY] * len(shapes),
        out_shape=[jax.ShapeDtypeStruct(s, F32) for s in shapes],
        scratch_shapes=[pltpu.SemaphoreType.DMA((len(plan),))],
        compiler_params=pltpu.CompilerParams(vmem_limit_bytes=16 << 20),
        cost_estimate=cost(1),
        name=name,
    )(*ins)


def flip(x, bits, cores=(0, 1)):
    n = lax.axis_size("leaf")
    return lax.ppermute(x, "leaf", [(i, i ^ bits) for i in range(n) if i % 2 in cores])


def swap(x, bit, cores=(0, 1)):
    return flip(x, 1 << bit, cores)


def shift(x, d):
    n = lax.axis_size("front")
    return lax.ppermute(x, "front", [(i, (i + d) % n) for i in range(n)])


def around(x):
    return [x, shift(x, 1), shift(x, -1), shift(x, 2)]


def after(x, *deps):
    return lax.optimization_barrier((x,) + deps)[0]


def body(leaf_update, sep1, rem1, sep2, rem2, sep3, rem3, map1, map2, map3):
    every = slice(None)
    at = lambda a, n: (slice(a, a + n), every)
    cut = lambda n, a=0, w=SEP: (slice(0, n), slice(a, a + w))
    e11_own, e21_own, e22_own, r2_own = copies(
        "cut",
        [(0, cut(64), 0, (every, every)), (1, cut(128), 1, at(0, 128)), (2, cut(32), 1, at(128, 32)),
         (3, cut(16), 1, at(160, 16)), (1, cut(128, SEP, UPD), 2, (every, every)),
         (4, cut(64), 3, at(0, 64)), (4, cut(64, SEP), 3, at(64, 64))],
        [sep1, rem1, sep2, sep3, rem2], [(64, SEP), (176, SEP), (128, UPD), (128, SEP)],
    )
    e11 = around(e11_own)
    u_sib = swap(leaf_update, 0)
    e21 = around(e21_own)
    g1 = lax.all_gather(e22_own, "front", axis=0, tiled=False)
    s21, s22 = spread(map1, leaf_update, u_sib)
    e11 = copies("join1", [(k, every, 0, at(64 * k, 64)) for k in range(4)], e11, [(256, SEP)])[0]
    e11_sw = swap(e11, 0)
    r2_sib = swap(after(r2_own, e11), 1)
    e11 = after(e11, s21, e21[1], e21[2])
    la, ta, fs, head = pivot_head(1, map1, [e11, e11_sw], [leaf_update, u_sib], [(SEP, SEP)] * 2)
    r2 = copies(
        "join2", [(0, (every, every), 0, (0, every, every)), (1, (every, every), 0, (1, every, every))],
        [r2_own, after(r2_sib, ta)], [(2, 128, SEP)],
    )[0]
    g2 = lax.all_gather(r2, "front", axis=0, tiled=False)
    lb, tb, out_p1 = pivot_tail(1, fs, head)
    e21 = e21[:1] + [after(x, tb) for x in e21[1:]]
    s3, t3 = copies(
        "join3",
        [(k, at(128, 48), 0, at(48 * k, 48)) for k in range(4)] + [(k, at(160, 16), 1, at(16 * k, 16)) for k in range(4)],
        e21, [(192, SEP), (64, SEP)],
    )
    s3_sib = swap(s3, 1)
    s3_sw = swap(s3, 0)
    e21 = [after(e21[0], s3)] + e21[1:]
    l21, out_b1 = solve_1((la, ta, lb, tb), s21, e21)
    other = swap(l21, 0)
    uhh = diag_1(l21, s22, after(g1, l21))
    z11 = swap(uhh, 1, (0,))
    uhh_sw = swap(uhh, 0)
    uba = cross_1(l21, after(other, uhh), s22, g1)
    s3_sib_sw = swap(after(s3_sib, uba), 0)
    z11 = after(z11, uba)
    z11_sw = swap(z11, 0)
    uba_sw = swap(uba, 0)
    zbb = swap(after(uhh, z11), 1, (1,))
    zba = swap(after(uba, z11), 1, (1,))
    s3 = [s3, s3_sib, s3_sw, s3_sib_sw]
    la, ta, fs, head = pivot_head(2, map2, s3, [uhh, uhh_sw, z11, z11_sw], [tiles_shape(10)] * 4)
    g2_sw = swap(after(g2, ta), 0)
    t3 = after(t3, ta)
    t3z = swap(t3, 2)
    t3zz = flip(t3, 6)
    lb, tb, out_p2 = pivot_tail(2, fs, head)
    zbb, zba, t3z, t3zz = lax.optimization_barrier((zbb, zba, t3z, t3zz, tb))[:4]
    factor = (la, ta, lb, tb)
    zbb_sw = swap(zbb, 0)
    zba_sw = swap(zba, 0)
    held = [uhh, uhh_sw, uba_sw, uba, uhh_sw, uhh, z11, z11_sw, zba_sw, zba, zbb_sw, zbb]
    l21a, v10, half = upper_2(map2, factor, held, g2, g2_sw)
    half_z = swap(half, 2)
    t3z_sw = swap(after(t3z, half), 0)
    t3zz_sw = swap(after(t3zz, half), 0)
    mine, send, out_b2 = lower_2(map2, map3, factor, l21a, v10, held[2:6] + held[8:], g2, g2_sw)
    half_z = after(half_z, mine)
    half_sw = swap(half_z, 0)
    got = swap(send, 2)
    s3 = s3 + [t3z, t3zz, t3z_sw, t3zz_sw]
    la, ta, fs, head = pivot_head(3, map3, s3, [v10, half_z, half_sw], [tiles_shape(n) for n in (10, 5, 5)])
    lb, tb, out_p3 = pivot_tail(3, fs, head)
    out_b3 = last((la, ta, lb, tb), rem3, mine, after(got, tb))
    return out_p1, out_b1, out_p2, out_b2, out_p3, out_b3


def solution(mesh):
    both = P(("leaf", "front"), None)
    in_specs = (P("leaf", None),) + (both,) * 6 + (P(), P(), P())
    return jax.shard_map(body, mesh=mesh, in_specs=in_specs, out_specs=(both,) * 6, check_vma=False)
```

```python
import functools
import jax
import jax.numpy as jnp
from jax import lax
from jax.experimental import pallas as pl
from jax.experimental.pallas import tpu as pltpu
from jax.sharding import PartitionSpec as P

TILE = 128
SEP = 512
UPD = 1024
F32 = jnp.float32
BF16 = jnp.bfloat16
AHEAD = 3
MAPS_AT = (0, 64, 96)
HALF = SEP // 2
ANY = pl.BlockSpec(memory_space=pl.ANY)
SMEM = pl.BlockSpec(memory_space=pltpu.SMEM)
VM = pltpu.VMEM
ROWS = (((1,), (1,)), ((), ()))


def params():
    return pltpu.CompilerParams(vmem_limit_bytes=56 << 20)


def cost(us):
    return pl.CostEstimate(flops=int(us * 1e6), bytes_accessed=int(us * 3e3), transcendentals=0)


def split(a):
    high = a.astype(BF16)
    return high, (a - high.astype(F32)).astype(BF16)


def dot_split(a, b):
    ah, al = a
    bh, bl = b
    mul = lambda x, y: lax.dot_general(x, y, ROWS, preferred_element_type=F32)
    return mul(ah, bh) + (mul(ah, bl) + mul(al, bh))


def dot_rows(a, b):
    return dot_split(split(a), split(b))


def lane(x, c):
    return jnp.broadcast_to(x[:, c : c + 1], (8, TILE))


def sublane(x, r):
    return jnp.broadcast_to(x[r : r + 1, :], (8, TILE))


def factor_tile(d_ref, w_ref):
    rows8 = lax.broadcasted_iota(jnp.int32, (8, TILE), 0)
    ri = lax.broadcasted_iota(jnp.int32, (TILE, TILE), 0)
    ci = lax.broadcasted_iota(jnp.int32, (TILE, TILE), 1)
    w_ref[...] = jnp.where(ri == ci, 1.0, 0.0).astype(F32)

    def pack(parts):
        out = parts[0]
        for t in range(1, 8):
            out = jnp.where(rows8 == t, parts[t], out)
        return out

    for q in range(16):
        o = 8 * q
        rows, inv = d_ref[o : o + 8, :], w_ref[o : o + 8, :]
        cols = [lane(rows, o + t) for t in range(8)]
        a = [[None] * 8 for _ in range(8)]
        for t in range(8):
            for s in range(t, 8):
                a[s][t] = sublane(cols[t], s)
        rs = [None] * 8
        low = [[None] * 8 for _ in range(8)]
        x_rows = [None] * 8
        v_rows = [None] * 8
        for t in range(0, 8, 2):
            aa, bb, cc = a[t][t], a[t + 1][t], a[t + 1][t + 1]
            rs[t] = lax.rsqrt(aa)
            rs[t + 1] = lax.rsqrt(aa * cc - bb * bb) * (aa * rs[t])
            low[t + 1][t] = bb * rs[t]
            for s in range(t + 2, 8):
                low[s][t] = a[s][t] * rs[t]
                low[s][t + 1] = (a[s][t + 1] - low[s][t] * low[t + 1][t]) * rs[t + 1]
            for s in range(t + 2, 8):
                for u in range(t + 2, s + 1):
                    a[s][u] = (a[s][u] - low[s][t] * low[u][t]) - low[s][t + 1] * low[u][t + 1]
        for t in range(8):
            x, v = sublane(rows, t), sublane(inv, t)
            for u in range(t):
                x = x - low[t][u] * x_rows[u]
                v = v - low[t][u] * v_rows[u]
            x_rows[t] = x * rs[t]
            v_rows[t] = v * rs[t]
        packed = pack(v_rows)
        w_ref[o : o + 8, :] = packed
        for po in [o + 8 * m for m in range(1, AHEAD + 1) if q + m < 16]:
            d_rows, w_rows = d_ref[po : po + 8, :], w_ref[po : po + 8, :]
            coef = [None] * 8
            for t in range(8):
                c = lane(d_rows, o + t)
                for u in range(t):
                    c = c - coef[u] * low[t][u]
                coef[t] = c * rs[t]
            for t in range(8):
                d_rows = d_rows - coef[t] * x_rows[t]
                w_rows = w_rows - coef[t] * v_rows[t]
            d_ref[po : po + 8, :] = d_rows
            w_ref[po : po + 8, :] = w_rows
        if q < 15 - AHEAD:
            both = jnp.concatenate([pack(x_rows), packed], axis=1)
            high = both.astype(BF16).astype(F32)
            rest = both - high
            left = jnp.concatenate([high[:, :TILE], high[:, :TILE], rest[:, :TILE]], axis=0)
            right = jnp.concatenate([high, rest, high], axis=0)
            prod = lax.dot_general(
                left.astype(BF16), right.astype(BF16), (((0,), (0,)), ((), ())), preferred_element_type=F32
            )
            po = o + 8 * (AHEAD + 1)
            d_ref[po:, :] = d_ref[po:, :] - prod[po:, :TILE]
            w_ref[po:, :] = w_ref[po:, :] - prod[po:, TILE:]


def places():
    return lax.axis_index("leaf"), lax.axis_index("front")


def block(i):
    return pl.ds(pl.multiple_of(i * TILE, TILE), TILE)


def vspec(shape):
    return pl.BlockSpec(shape, lambda i: (0,) * len(shape))


def tiles_shape(n):
    return (n, TILE, TILE)


def call(kernel, name, us, ins, in_specs, outs, scratch):
    return pl.pallas_call(
        kernel,
        grid=(1,),
        in_specs=in_specs,
        out_specs=[vspec(s) for s, _ in outs],
        out_shape=[jax.ShapeDtypeStruct(s, t) for s, t in outs],
        scratch_shapes=scratch,
        compiler_params=params(),
        cost_estimate=cost(us),
        name=name,
    )(*ins)


def scatter(dst_ref, maps_ref, child, get_tile, rows, row_lo):
    for i in rows:
        mi = maps_ref[child, i] - row_lo

        @pl.when((mi >= 0) & (mi < 4))
        def _(i=i, mi=mi):
            for j in range(i + 1):
                dst_ref[block(mi), block(maps_ref[child, j])] += get_tile(i, j)


def tri(i, j):
    return i * (i + 1) // 2 + j


def pivot_head_kernel(level, maps_ref, *refs):
    n_pieces = (2, 2, 4)[level - 1]
    pieces, tiles = refs[:n_pieces], refs[n_pieces : len(refs) - 7]
    l_ref, t_ref, fs_ref, own_ref, f, d, w = refs[len(refs) - 7 :]
    leaf, y = places()
    core = leaf & 1
    n = SEP // (4 * 2**level)

    def put(ref, start, who, y_rel):
        pos = (who & (2**level - 1)) * 4 + ((y + y_rel) & 3)
        f[pl.ds(pl.multiple_of(pos * n, n), n), :] = ref[start : start + n, :]

    for i, rel in enumerate((0, 3, 1, 2)):
        for core_rel in range(2):
            who = leaf ^ core_rel
            if level == 1:
                put(pieces[core_rel], 64 * i, who, rel)
                continue
            for z1 in range(2):
                ref, at_z1, base = pieces[core_rel], who ^ (z1 << 1), 96 * i + 48 * z1
                if level == 2:
                    put(ref, base, at_z1, rel)
                else:
                    put(ref, base + 32, at_z1, rel)
                    put(pieces[2 + core_rel], 32 * i + 16 * z1, at_z1 ^ 4, rel)

    first = MAPS_AT[level - 1]
    own = first + (leaf >> (level - 1))
    sib = first + ((leaf >> (level - 1)) ^ 1)
    rows = range(4)
    if level == 1:
        for child, ref in ((own, tiles[0]), (sib, tiles[1])):
            scatter(f, maps_ref, child, lambda i, j, ref=ref: ref[tile_at(i), tile_at(j)], rows, 0)
    else:
        for c in range(2):

            @pl.when(core == c)
            def _(c=c):
                if level == 2:
                    for child, ref in ((own, tiles[c]), (sib, tiles[2 + c])):
                        scatter(f, maps_ref, child, lambda i, j, ref=ref: ref[tri(i, j)], rows, 0)
                else:
                    pair = (tiles[1 + c], tiles[2 - c])
                    scatter(f, maps_ref, own, lambda i, j: tiles[0][tri(i, j)], rows, 0)
                    scatter(f, maps_ref, sib, lambda i, j: pair[tri(i, j) // 5][tri(i, j) % 5], rows, 0)

    factor_pair(f, l_ref, t_ref, d, w, SEP)
    fs_ref[...] = f[HALF:, HALF:]
    pos = (leaf & (2**level - 1)) * 4 + y
    own_ref[...] = l_ref[pl.ds(pl.multiple_of(pos * n, n), n), :]


def tile_at(i):
    return slice(i * TILE, (i + 1) * TILE)


def factor_pair(f, l_ref, t_ref, d, w, order):
    ri = lax.broadcasted_iota(jnp.int32, (TILE, TILE), 0)
    ci = lax.broadcasted_iota(jnp.int32, (TILE, TILE), 1)
    for b in range(2):
        o = b * TILE
        d[...] = f[o : o + TILE, o : o + TILE]
        factor_tile(d, w)
        t_ref[b] = w[...]
        panel = dot_rows(f[o:order, o : o + TILE], w[...])
        if b:
            l_ref[:TILE, o : o + TILE] = jnp.zeros((TILE, TILE), F32)
        l_ref[o : o + TILE, o : o + TILE] = jnp.where(ri >= ci, panel[:TILE], 0.0)
        if o + TILE == order:
            continue
        below = panel[TILE:]
        l_ref[o + TILE :, o : o + TILE] = below
        high, low = split(below)
        for c in range(b + 1, order // TILE):
            k = (c - b - 1) * TILE
            at = slice(c * TILE, order)
            prod = dot_split((high[k:], low[k:]), (high[k : k + TILE], low[k : k + TILE]))
            f[at, tile_at(c)] = f[at, tile_at(c)] - prod


def pivot_tail_kernel(level, fs_ref, head_ref, l_ref, t_ref, own_ref, f, d, w):
    leaf, y = places()
    n = SEP // (4 * 2**level)
    f[...] = fs_ref[...]
    factor_pair(f, l_ref, t_ref, d, w, HALF)
    pos = ((leaf & (2**level - 1)) * 4 + y) * n
    own_ref[:, :HALF] = head_ref[...]

    @pl.when(pos < HALF)
    def _():
        own_ref[:, HALF:] = jnp.zeros((n, HALF), F32)

    @pl.when(pos >= HALF)
    def _():
        own_ref[:, HALF:] = l_ref[pl.ds(pl.multiple_of(pos - HALF, n), n), :]


def pivot_head(level, maps, pieces, tiles, tile_shapes):
    n = SEP // (4 * 2**level)
    return call(
        functools.partial(pivot_head_kernel, level), "pivot_head%d" % level, 11,
        [maps, *pieces, *tiles],
        [SMEM] + [vspec(p.shape) for p in pieces] + [vspec(s) for s in tile_shapes],
        [((SEP, HALF), F32), (tiles_shape(2), F32), ((HALF, HALF), F32), ((n, HALF), F32)],
        [VM((SEP, SEP), F32), VM((TILE, TILE), F32), VM((TILE, TILE), F32)],
    )


def pivot_tail(level, fs, head):
    n = SEP // (4 * 2**level)
    return call(
        functools.partial(pivot_tail_kernel, level), "pivot_tail%d" % level, 9,
        [fs, head], [vspec((HALF, HALF)), vspec((n, HALF))],
        [((HALF, HALF), F32), (tiles_shape(2), F32), ((n, SEP), F32)],
        [VM((HALF, HALF), F32), VM((TILE, TILE), F32), VM((TILE, TILE), F32)],
    )


FACTOR = [vspec((SEP, HALF)), vspec(tiles_shape(2)), vspec((HALF, HALF)), vspec(tiles_shape(2))]


def solve_rows(get, factor, out_ref):
    la, ta, lb, tb = factor
    high, low = [], []
    for b in range(4):
        cols = get(b)
        for c in range(b):
            ref, rr, cc = (la, b, c) if c < 2 else (lb, b - 2, c - 2)
            cols = cols - dot_split((high[c], low[c]), split(ref[tile_at(rr), tile_at(cc)]))
        part = dot_rows(cols, (ta if b < 2 else tb)[b % 2])
        out_ref[:, tile_at(b)] = part
        ph, plo = split(part)
        high.append(ph)
        low.append(plo)
    return jnp.concatenate(high, axis=1), jnp.concatenate(low, axis=1)


def emit_lower(done, get, u_ref):
    for i in range(4):
        wide = (i + 1) * TILE
        prod = dot_split((done[0][tile_at(i)], done[1][tile_at(i)]), (done[0][:wide], done[1][:wide]))
        for j in range(i + 1):
            u_ref[tri(i, j)] = get(i, j) - prod[:, tile_at(j)]


def spread_kernel(maps_ref, own_ref, sib_ref, s21, s22, dst):
    leaf, _ = places()
    row_lo = 4 + 4 * (leaf & 1)
    dst[...] = jnp.zeros_like(dst)
    for child, ref in ((leaf, own_ref), (leaf ^ 1, sib_ref)):
        scatter(dst, maps_ref, child, lambda i, j, ref=ref: ref[tile_at(i), tile_at(j)], range(8), row_lo)
    s21[...] = dst[:, :SEP]
    s22[...] = dst[:, SEP:]


def spread(maps, own, sib):
    return call(
        spread_kernel, "spread", 7, [maps, own, sib], [SMEM, vspec((UPD, UPD)), vspec((UPD, UPD))],
        [((SEP, SEP), F32), ((SEP, UPD), F32)], [VM((SEP, SEP + UPD), F32)],
    )


def solve_kernel_1(la, ta, lb, tb, s21, e0, e1, e2, e3, l21_ref, below_ref, x):
    _, y = places()
    x[...] = s21[...]
    for ref, rel in ((e0, 0), (e1, 3), (e2, 1), (e3, 2)):
        x[block((y + rel) & 3), :] += ref[...]
    solve_rows(lambda b: x[:, tile_at(b)], (la, ta, lb, tb), l21_ref)
    below_ref[...] = l21_ref[block(y), :]


def solve_1(factor, s21, pieces):
    return call(
        solve_kernel_1, "solve1", 4, [*factor, s21, *pieces],
        FACTOR + [vspec((SEP, SEP))] + [vspec((TILE, SEP))] * 4,
        [((SEP, SEP), F32), ((TILE, SEP), F32)], [VM((SEP, SEP), F32)],
    )


def diag_kernel_1(l21_ref, s22, g_ref, u_ref, e, t, sem):
    leaf, _ = places()
    at = pl.ds(pl.multiple_of((leaf & 1) * SEP, SEP), SEP)
    first = pltpu.make_async_copy(g_ref.at[:, :, at], e, sem.at[0])
    second = pltpu.make_async_copy(s22.at[:, at], t, sem.at[1])
    first.start()
    second.start()
    done = split(l21_ref[...])
    first.wait()
    second.wait()
    emit_lower(done, lambda i, j: e[i, :, tile_at(j)] + t[tile_at(i), tile_at(j)], u_ref)


def diag_1(l21, s22, g1):
    return call(
        diag_kernel_1, "diag1", 4, [l21, s22, g1], [vspec((SEP, SEP)), ANY, ANY],
        [(tiles_shape(10), F32)],
        [VM((4, TILE, SEP), F32), VM((SEP, SEP), F32), pltpu.SemaphoreType.DMA((2,))],
    )[0]


def cross_kernel_1(l21_ref, other_ref, s22, g_ref, u_ref, e, t, sem):
    leaf, _ = places()
    at = pl.ds(0, SEP)
    first = pltpu.make_async_copy(g_ref.at[:, :, at], e, sem.at[0])
    second = pltpu.make_async_copy(s22.at[:, at], t, sem.at[1])
    first.start()
    second.start()
    first.wait()
    second.wait()

    @pl.when((leaf & 1) == 1)
    def _():
        top = split(other_ref[...])
        for i in range(4):
            prod = dot_split(split(l21_ref[tile_at(i), :]), top)
            for j in range(4):
                u_ref[4 * i + j] = (e[i, :, tile_at(j)] + t[tile_at(i), tile_at(j)]) - prod[:, tile_at(j)]


def cross_1(l21, other, s22, g1):
    return call(
        cross_kernel_1, "cross1", 5, [l21, other, s22, g1], [vspec((SEP, SEP)), vspec((SEP, SEP)), ANY, ANY],
        [(tiles_shape(16), F32)],
        [VM((4, TILE, SEP), F32), VM((SEP, SEP), F32), pltpu.SemaphoreType.DMA((2,))],
    )[0]


def load_tiles(pairs, core, bufs, sem):
    for k, (pair, buf) in enumerate(zip(pairs, bufs)):
        for c in range(2):

            @pl.when(core == c)
            def _(pair=pair, buf=buf, c=c, k=k):
                pltpu.make_async_copy(pair[c], buf, sem.at[k]).start()

    return [pltpu.make_async_copy(pair[0], buf, sem.at[k]) for k, (pair, buf) in enumerate(zip(pairs, bufs))]


def load_rows_2(which, g_own, g_sw, e, sem, base):
    leaf, _ = places()
    core = leaf & 1
    z_rel = ((leaf >> 1) & 1) ^ which
    copies = []
    for y in range(4):
        for part in range(2):
            for src, who in ((g_own, core), (g_sw, 1 - core)):
                row = pl.multiple_of(who * 256 + y * 64, 64)
                dst = e.at[pl.ds(row, 64), part * SEP : (part + 1) * SEP]
                copies.append(pltpu.make_async_copy(src.at[y, z_rel, part * 64 : (part + 1) * 64], dst, sem.at[base + len(copies)]))
    for c in copies:
        c.start()
    return copies


def tile_getter(t11, tba, tbb):
    def get(i, j):
        if i < 4:
            return t11[tri(i, j)]
        if j < 4:
            return tba[4 * (i - 4) + j]
        return tbb[tri(i - 4, j - 4)]

    return get


def upper_kernel_2(maps_ref, la, ta, lb, tb, *refs):
    held, (g_own, g_sw, l21_ref, u_ref, half_ref, e, sem), bufs = refs[:12], refs[12:19], refs[19:]
    leaf, _ = places()
    core = leaf & 1
    copies = load_rows_2(0, g_own, g_sw, e, sem, 6)
    copies += load_tiles([(held[2 * k], held[2 * k + 1]) for k in range(6)], core, bufs, sem)
    for c in copies:
        c.wait()
    own = MAPS_AT[1] + (leaf >> 1)
    scatter(e, maps_ref, own, tile_getter(*bufs[:3]), range(7), 4)
    scatter(e, maps_ref, own ^ 1, tile_getter(*bufs[3:]), range(7), 4)
    done = solve_rows(lambda b: e[:, tile_at(b)], (la, ta, lb, tb), l21_ref)
    emit_lower(done, lambda i, j: e[tile_at(i), tile_at(4 + j)], u_ref)
    half_ref[...] = u_ref[pl.ds(core * 5, 5)]


def upper_2(maps, factor, held, g_own, g_sw):
    return call(
        upper_kernel_2, "upper2", 9, [maps, *factor, *held, g_own, g_sw],
        [SMEM] + FACTOR + [ANY] * 14,
        [((SEP, SEP), F32), (tiles_shape(10), F32), (tiles_shape(5), F32)],
        [VM((SEP, UPD), F32), pltpu.SemaphoreType.DMA((22,))] + [VM(tiles_shape(n), F32) for n in (10, 16, 10) * 2],
    )


def lower_kernel_2(maps_ref, la, ta, lb, tb, l21a, u10, *refs):
    held, (g_own, g_sw, mine_ref, send_ref, below_ref, e, l21b, u21, sem), bufs = refs[:8], refs[8:17], refs[17:]
    leaf, y = places()
    core = leaf & 1
    e[:, UPD:] = jnp.zeros((SEP, SEP), F32)
    copies = load_rows_2(1, g_own, g_sw, e, sem, 4)
    copies += load_tiles([(held[2 * k], held[2 * k + 1]) for k in range(4)], core, bufs, sem)
    for c in copies:
        c.wait()
    own = MAPS_AT[1] + (leaf >> 1)
    scatter(e, maps_ref, own, tile_getter(None, *bufs[:2]), range(4, 8), 8)
    scatter(e, maps_ref, own ^ 1, tile_getter(None, *bufs[2:]), range(4, 8), 8)
    done = solve_rows(lambda b: e[:, tile_at(b)], (la, ta, lb, tb), l21b)
    u21[...] = e[:, SEP:UPD] - dot_split(done, split(l21a[...]))
    child = MAPS_AT[2] + (leaf >> 2)
    stripe = pl.ds(pl.multiple_of(y * 32, 32), 32)
    for out_ref, who in ((mine_ref, leaf), (send_ref, leaf ^ 4)):
        out_ref[...] = jnp.zeros_like(out_ref)
        want = 4 + (who & 7)
        for j in range(1, 8):

            @pl.when(maps_ref[child, j] == want)
            def _(j=j, out_ref=out_ref):
                for c in range(min(j, 4)):
                    mj = maps_ref[child, c]

                    @pl.when(mj < 4)
                    def _(c=c, mj=mj):
                        if j < 4:
                            piece = u10[tri(j, c), stripe, :]
                        else:
                            row = pl.multiple_of((j - 4) * TILE + y * 32, 32)
                            piece = u21[pl.ds(row, 32), tile_at(c)]
                        out_ref[:, block(mj)] = piece

    pos = ((leaf & 3) * 4 + y) * 64

    @pl.when(pos < SEP)
    def _():
        below_ref[...] = l21a[pl.ds(pl.multiple_of(pos, 64), 64), :]

    @pl.when(pos >= SEP)
    def _():
        below_ref[...] = l21b[pl.ds(pl.multiple_of(pos - SEP, 64), 64), :]


def lower_2(maps, factor, l21a, u10, held, g_own, g_sw):
    return call(
        lower_kernel_2, "lower2", 9, [maps, *factor, l21a, u10, *held, g_own, g_sw],
        [SMEM] + FACTOR + [vspec((SEP, SEP)), vspec(tiles_shape(10))] + [ANY] * 10,
        [((32, SEP), F32), ((32, SEP), F32), ((64, SEP), F32)],
        [VM((SEP, SEP + UPD), F32), VM((SEP, SEP), F32), VM((SEP, SEP), F32), pltpu.SemaphoreType.DMA((20,))]
        + [VM(tiles_shape(n), F32) for n in (16, 10) * 2],
    )


def last_kernel(la, ta, lb, tb, e_ref, mine_ref, got_ref, out_ref):
    x = e_ref[...] + mine_ref[...] + got_ref[...]
    solve_rows(lambda b: x[:, tile_at(b)], (la, ta, lb, tb), out_ref)


def last(factor, rem3, mine, got):
    return call(
        last_kernel, "last", 3, [*factor, rem3, mine, got], FACTOR + [vspec((32, SEP))] * 3, [((32, SEP), F32)], []
    )[0]


def copy_kernel(plan, n_in, *refs):
    ins, outs, sem = refs[:n_in], refs[n_in:-1], refs[-1]
    copies = []
    for k, (src, src_at, dst, dst_at) in enumerate(plan):
        copies.append(pltpu.make_async_copy(ins[src].at[src_at], outs[dst].at[dst_at], sem.at[k]))
    for c in copies:
        c.start()
    for c in copies:
        c.wait()


def copies(name, plan, ins, shapes):
    return pl.pallas_call(
        functools.partial(copy_kernel, plan, len(ins)),
        in_specs=[ANY] * len(ins),
        out_specs=[ANY] * len(shapes),
        out_shape=[jax.ShapeDtypeStruct(s, F32) for s in shapes],
        scratch_shapes=[pltpu.SemaphoreType.DMA((len(plan),))],
        compiler_params=params(),
        cost_estimate=cost(1),
        name=name,
    )(*ins)


def flip(x, bits, cores=(0, 1)):
    n = lax.axis_size("leaf")
    return lax.ppermute(x, "leaf", [(i, i ^ bits) for i in range(n) if i % 2 in cores])


def swap(x, bit, cores=(0, 1)):
    return flip(x, 1 << bit, cores)


def shift(x, d):
    n = lax.axis_size("front")
    return lax.ppermute(x, "front", [(i, (i + d) % n) for i in range(n)])


def around(x):
    return [x, shift(x, 1), shift(x, -1), shift(x, 2)]


def after(x, *deps):
    return lax.optimization_barrier((x,) + deps)[0]


def body(leaf_update, sep1, rem1, sep2, rem2, sep3, rem3, map1, map2, map3):
    every = slice(None)
    whole = (every, every)
    at = lambda a, n: (slice(a, a + n), every)
    cut = lambda n, a=0, w=SEP: (slice(0, n), slice(a, a + w))
    maps = jnp.concatenate([map1, map2, map3], axis=0)
    e11_own, e21_own, s_own, e22_own, r2_own = copies(
        "cut",
        [(0, cut(64), 0, whole), (1, cut(128), 1, whole), (2, cut(32), 2, at(0, 32)), (3, cut(16), 2, at(32, 16)),
         (1, cut(128, SEP, UPD), 3, whole), (4, cut(64), 4, at(0, 64)), (4, cut(64, SEP), 4, at(64, 64))],
        [sep1, rem1, sep2, sep3, rem2], [(64, SEP), (128, SEP), (48, SEP), (128, UPD), (128, SEP)],
    )
    e11 = around(e11_own)
    s_sib = swap(s_own, 1)
    u_sib = swap(leaf_update, 0)
    g1 = lax.all_gather(e22_own, "front", axis=0, tiled=False)
    s21, s22 = spread(maps, leaf_update, u_sib)
    e11[1] = after(e11[1], s_sib)
    e11 = copies("join1", [(k, every, 0, at(64 * k, 64)) for k in range(4)], e11, [(256, SEP)])[0]
    e11_sw = swap(e11, 0)
    e21_own = copies(
        "join2", [(0, whole, 0, at(0, 128)), (1, whole, 0, at(128, 48)), (2, whole, 0, at(176, 48))],
        [e21_own, s_own, after(s_sib, e11)], [(224, SEP)],
    )[0]
    e21 = around(e21_own)
    r2_sib = swap(after(r2_own, e11), 1)
    e11 = after(e11, s21)
    la, ta, fs, head = pivot_head(1, maps, [e11, e11_sw], [leaf_update, u_sib], [(SEP, SEP)] * 2)
    r2_sib, e21[1], e21[2] = lax.optimization_barrier((r2_sib, e21[1], e21[2], ta))[:3]
    r2 = copies(
        "join3", [(0, whole, 0, (0, every, every)), (1, whole, 0, (1, every, every))], [r2_own, r2_sib], [(2, 128, SEP)]
    )[0]
    g2 = lax.all_gather(r2, "front", axis=0, tiled=False)
    lb, tb, out_p1 = pivot_tail(1, fs, head)
    e21[3] = after(e21[3], tb)
    l21, out_b1 = solve_1((la, ta, lb, tb), s21, e21)
    other = swap(l21, 0)
    uhh = diag_1(l21, s22, after(g1, l21))
    z11 = swap(uhh, 1, (0,))
    uhh_sw = swap(uhh, 0)
    uba = cross_1(l21, after(other, uhh), s22, g1)
    s3, t3 = copies(
        "join4",
        [(k, at(128, 96), 0, at(96 * k, 96)) for k in range(4)]
        + [(k, at(160 + 48 * z, 16), 1, at(32 * k + 16 * z, 16)) for k in range(4) for z in range(2)],
        [after(e21[0], uba)] + e21[1:], [(384, SEP), (128, SEP)],
    )
    s3_sw = swap(s3, 0)
    z11 = after(z11, s3)
    z11_sw = swap(z11, 0)
    uba_sw = swap(uba, 0)
    zbb = swap(after(uhh, z11), 1, (1,))
    zba = swap(after(uba, z11), 1, (1,))
    la, ta, fs, head = pivot_head(2, maps, [s3, s3_sw], [uhh, uhh_sw, z11, z11_sw], [tiles_shape(10)] * 4)
    g2_sw = swap(after(g2, ta), 0)
    t3z = swap(after(t3, ta), 2)
    lb, tb, out_p2 = pivot_tail(2, fs, head)
    zbb, zba, t3z = lax.optimization_barrier((zbb, zba, t3z, tb))[:3]
    factor = (la, ta, lb, tb)
    zbb_sw = swap(zbb, 0)
    zba_sw = swap(zba, 0)
    held = [uhh, uhh_sw, uba_sw, uba, uhh_sw, uhh, z11, z11_sw, zba_sw, zba, zbb_sw, zbb]
    l21a, v10, half = upper_2(maps, factor, held, g2, g2_sw)
    half_z = swap(half, 2)
    t3z_sw = swap(after(t3z, half), 0)
    mine, send, out_b2 = lower_2(maps, factor, l21a, v10, held[2:6] + held[8:], g2, g2_sw)
    half_z = after(half_z, mine)
    half_sw = swap(half_z, 0)
    got = swap(send, 2)
    s3 = [s3, s3_sw, t3z, t3z_sw]
    la, ta, fs, head = pivot_head(3, maps, s3, [v10, half_z, half_sw], [tiles_shape(n) for n in (10, 5, 5)])
    lb, tb, out_p3 = pivot_tail(3, fs, head)
    out_b3 = last((la, ta, lb, tb), rem3, mine, after(got, tb))
    return out_p1, out_b1, out_p2, out_b2, out_p3, out_b3


def solution(mesh):
    both = P(("leaf", "front"), None)
    in_specs = (P("leaf", None),) + (both,) * 6 + (P(), P(), P())
    return jax.shard_map(body, mesh=mesh, in_specs=in_specs, out_specs=(both,) * 6, check_vma=False)
```

```python
import functools
import jax
import jax.numpy as jnp
from jax import lax
from jax.experimental import pallas as pl
from jax.experimental.pallas import tpu as pltpu
from jax.sharding import PartitionSpec as P

TILE = 128
SEP = 512
UPD = 1024
F32 = jnp.float32
BF16 = jnp.bfloat16
AHEAD = 3
MAPS_AT = (0, 64, 96)
HALF = SEP // 2
ANY = pl.BlockSpec(memory_space=pl.ANY)
SMEM = pl.BlockSpec(memory_space=pltpu.SMEM)
VM = pltpu.VMEM
ROWS = (((1,), (1,)), ((), ()))


def params():
    return pltpu.CompilerParams(vmem_limit_bytes=56 << 20)


def cost(us):
    return pl.CostEstimate(flops=int(us * 1e6), bytes_accessed=int(us * 3e3), transcendentals=0)


def split(a):
    high = a.astype(BF16)
    return high, (a - high.astype(F32)).astype(BF16)


def dot_split(a, b):
    ah, al = a
    bh, bl = b
    mul = lambda x, y: lax.dot_general(x, y, ROWS, preferred_element_type=F32)
    return mul(ah, bh) + (mul(ah, bl) + mul(al, bh))


def dot_rows(a, b):
    return dot_split(split(a), split(b))


def lane(x, c):
    return jnp.broadcast_to(x[:, c : c + 1], (8, TILE))


def sublane(x, r):
    return jnp.broadcast_to(x[r : r + 1, :], (8, TILE))


def factor_tile(d_ref, w_ref):
    rows8 = lax.broadcasted_iota(jnp.int32, (8, TILE), 0)
    ri = lax.broadcasted_iota(jnp.int32, (TILE, TILE), 0)
    ci = lax.broadcasted_iota(jnp.int32, (TILE, TILE), 1)
    w_ref[...] = jnp.where(ri == ci, 1.0, 0.0).astype(F32)

    def pack(parts):
        out = parts[0]
        for t in range(1, 8):
            out = jnp.where(rows8 == t, parts[t], out)
        return out

    for q in range(16):
        o = 8 * q
        rows, inv = d_ref[o : o + 8, :], w_ref[o : o + 8, :]
        cols = [lane(rows, o + t) for t in range(8)]
        a = [[None] * 8 for _ in range(8)]
        for t in range(8):
            for s in range(t, 8):
                a[s][t] = sublane(cols[t], s)
        rs = [None] * 8
        low = [[None] * 8 for _ in range(8)]
        x_rows = [None] * 8
        v_rows = [None] * 8
        for t in range(0, 8, 2):
            aa, bb, cc = a[t][t], a[t + 1][t], a[t + 1][t + 1]
            rs[t] = lax.rsqrt(aa)
            rs[t + 1] = lax.rsqrt(aa * cc - bb * bb) * (aa * rs[t])
            low[t + 1][t] = bb * rs[t]
            for s in range(t + 2, 8):
                low[s][t] = a[s][t] * rs[t]
                low[s][t + 1] = (a[s][t + 1] - low[s][t] * low[t + 1][t]) * rs[t + 1]
            for s in range(t + 2, 8):
                for u in range(t + 2, s + 1):
                    a[s][u] = (a[s][u] - low[s][t] * low[u][t]) - low[s][t + 1] * low[u][t + 1]
        for t in range(8):
            x, v = sublane(rows, t), sublane(inv, t)
            for u in range(t):
                x = x - low[t][u] * x_rows[u]
                v = v - low[t][u] * v_rows[u]
            x_rows[t] = x * rs[t]
            v_rows[t] = v * rs[t]
        packed = pack(v_rows)
        w_ref[o : o + 8, :] = packed
        for po in [o + 8 * m for m in range(1, AHEAD + 1) if q + m < 16]:
            d_rows, w_rows = d_ref[po : po + 8, :], w_ref[po : po + 8, :]
            coef = [None] * 8
            for t in range(8):
                c = lane(d_rows, o + t)
                for u in range(t):
                    c = c - coef[u] * low[t][u]
                coef[t] = c * rs[t]
            for t in range(8):
                d_rows = d_rows - coef[t] * x_rows[t]
                w_rows = w_rows - coef[t] * v_rows[t]
            d_ref[po : po + 8, :] = d_rows
            w_ref[po : po + 8, :] = w_rows
        if q < 15 - AHEAD:
            both = jnp.concatenate([pack(x_rows), packed], axis=1)
            high = both.astype(BF16).astype(F32)
            rest = both - high
            left = jnp.concatenate([high[:, :TILE], high[:, :TILE], rest[:, :TILE]], axis=0)
            right = jnp.concatenate([high, rest, high], axis=0)
            prod = lax.dot_general(
                left.astype(BF16), right.astype(BF16), (((0,), (0,)), ((), ())), preferred_element_type=F32
            )
            po = o + 8 * (AHEAD + 1)
            d_ref[po:, :] = d_ref[po:, :] - prod[po:, :TILE]
            w_ref[po:, :] = w_ref[po:, :] - prod[po:, TILE:]


def places():
    return lax.axis_index("leaf"), lax.axis_index("front")


def block(i):
    return pl.ds(pl.multiple_of(i * TILE, TILE), TILE)


def vspec(shape):
    return pl.BlockSpec(shape, lambda i: (0,) * len(shape))


def tiles_shape(n):
    return (n, TILE, TILE)


def call(kernel, name, us, ins, in_specs, outs, scratch):
    return pl.pallas_call(
        kernel,
        grid=(1,),
        in_specs=in_specs,
        out_specs=[vspec(s) for s, _ in outs],
        out_shape=[jax.ShapeDtypeStruct(s, t) for s, t in outs],
        scratch_shapes=scratch,
        compiler_params=params(),
        cost_estimate=cost(us),
        name=name,
    )(*ins)


def scatter(dst_ref, maps_ref, child, get_tile, rows, row_lo):
    for i in rows:
        mi = maps_ref[child, i] - row_lo

        @pl.when((mi >= 0) & (mi < 4))
        def _(i=i, mi=mi):
            for j in range(i + 1):
                dst_ref[block(mi), block(maps_ref[child, j])] += get_tile(i, j)


def tri(i, j):
    return i * (i + 1) // 2 + j


def pivot_head_kernel(level, maps_ref, *refs):
    n_pieces = (2, 2, 4)[level - 1]
    pieces, tiles = refs[:n_pieces], refs[n_pieces : len(refs) - 7]
    l_ref, t_ref, fs_ref, own_ref, f, d, w = refs[len(refs) - 7 :]
    leaf, y = places()
    core = leaf & 1
    n = SEP // (4 * 2**level)

    def put(ref, start, who, y_rel):
        pos = (who & (2**level - 1)) * 4 + ((y + y_rel) & 3)
        f[pl.ds(pl.multiple_of(pos * n, n), n), :] = ref[start : start + n, :]

    for i, rel in enumerate((0, 3, 1, 2)):
        for core_rel in range(2):
            who = leaf ^ core_rel
            if level == 1:
                put(pieces[core_rel], 64 * i, who, rel)
                continue
            for z1 in range(2):
                ref, at_z1, base = pieces[core_rel], who ^ (z1 << 1), 96 * i + 48 * z1
                if level == 2:
                    put(ref, base, at_z1, rel)
                else:
                    put(ref, base + 32, at_z1, rel)
                    put(pieces[2 + core_rel], 32 * i + 16 * z1, at_z1 ^ 4, rel)

    first = MAPS_AT[level - 1]
    own = first + (leaf >> (level - 1))
    sib = first + ((leaf >> (level - 1)) ^ 1)
    rows = range(4)
    if level == 1:
        for child, ref in ((own, tiles[0]), (sib, tiles[1])):
            scatter(f, maps_ref, child, lambda i, j, ref=ref: ref[tile_at(i), tile_at(j)], rows, 0)
    else:
        for c in range(2):

            @pl.when(core == c)
            def _(c=c):
                if level == 2:
                    for child, ref in ((own, tiles[c]), (sib, tiles[2 + c])):
                        scatter(f, maps_ref, child, lambda i, j, ref=ref: ref[tri(i, j)], rows, 0)
                else:
                    pair = (tiles[1 + c], tiles[2 - c])
                    scatter(f, maps_ref, own, lambda i, j: tiles[0][tri(i, j)], rows, 0)
                    scatter(f, maps_ref, sib, lambda i, j: pair[tri(i, j) // 5][tri(i, j) % 5], rows, 0)

    factor_pair(f, l_ref, t_ref, d, w, SEP)
    fs_ref[...] = f[HALF:, HALF:]
    pos = (leaf & (2**level - 1)) * 4 + y
    own_ref[...] = l_ref[pl.ds(pl.multiple_of(pos * n, n), n), :]


def tile_at(i):
    return slice(i * TILE, (i + 1) * TILE)


def factor_pair(f, l_ref, t_ref, d, w, order):
    ri = lax.broadcasted_iota(jnp.int32, (TILE, TILE), 0)
    ci = lax.broadcasted_iota(jnp.int32, (TILE, TILE), 1)
    for b in range(2):
        o = b * TILE
        d[...] = f[o : o + TILE, o : o + TILE]
        factor_tile(d, w)
        t_ref[b] = w[...]
        panel = dot_rows(f[o:order, o : o + TILE], w[...])
        if b:
            l_ref[:TILE, o : o + TILE] = jnp.zeros((TILE, TILE), F32)
        l_ref[o : o + TILE, o : o + TILE] = jnp.where(ri >= ci, panel[:TILE], 0.0)
        if o + TILE == order:
            continue
        below = panel[TILE:]
        l_ref[o + TILE :, o : o + TILE] = below
        high, low = split(below)
        for c in range(b + 1, order // TILE):
            k = (c - b - 1) * TILE
            at = slice(c * TILE, order)
            prod = dot_split((high[k:], low[k:]), (high[k : k + TILE], low[k : k + TILE]))
            f[at, tile_at(c)] = f[at, tile_at(c)] - prod


def pivot_tail_kernel(level, fs_ref, head_ref, l_ref, t_ref, own_ref, f, d, w):
    leaf, y = places()
    n = SEP // (4 * 2**level)
    f[...] = fs_ref[...]
    factor_pair(f, l_ref, t_ref, d, w, HALF)
    pos = ((leaf & (2**level - 1)) * 4 + y) * n
    own_ref[:, :HALF] = head_ref[...]

    @pl.when(pos < HALF)
    def _():
        own_ref[:, HALF:] = jnp.zeros((n, HALF), F32)

    @pl.when(pos >= HALF)
    def _():
        own_ref[:, HALF:] = l_ref[pl.ds(pl.multiple_of(pos - HALF, n), n), :]


def pivot_head(level, maps, pieces, tiles, tile_shapes):
    n = SEP // (4 * 2**level)
    return call(
        functools.partial(pivot_head_kernel, level), "pivot_head%d" % level, 11,
        [maps, *pieces, *tiles],
        [SMEM] + [vspec(p.shape) for p in pieces] + [vspec(s) for s in tile_shapes],
        [((SEP, HALF), F32), (tiles_shape(2), F32), ((HALF, HALF), F32), ((n, HALF), F32)],
        [VM((SEP, SEP), F32), VM((TILE, TILE), F32), VM((TILE, TILE), F32)],
    )


def pivot_tail(level, fs, head):
    n = SEP // (4 * 2**level)
    return call(
        functools.partial(pivot_tail_kernel, level), "pivot_tail%d" % level, 9,
        [fs, head], [vspec((HALF, HALF)), vspec((n, HALF))],
        [((HALF, HALF), F32), (tiles_shape(2), F32), ((n, SEP), F32)],
        [VM((HALF, HALF), F32), VM((TILE, TILE), F32), VM((TILE, TILE), F32)],
    )


FACTOR = [vspec((SEP, HALF)), vspec(tiles_shape(2)), vspec((HALF, HALF)), vspec(tiles_shape(2))]


def solve_rows(get, factor, out_ref):
    la, ta, lb, tb = factor
    high, low = [], []
    for b in range(4):
        cols = get(b)
        for c in range(b):
            ref, rr, cc = (la, b, c) if c < 2 else (lb, b - 2, c - 2)
            cols = cols - dot_split((high[c], low[c]), split(ref[tile_at(rr), tile_at(cc)]))
        part = dot_rows(cols, (ta if b < 2 else tb)[b % 2])
        out_ref[:, tile_at(b)] = part
        ph, plo = split(part)
        high.append(ph)
        low.append(plo)
    return jnp.concatenate(high, axis=1), jnp.concatenate(low, axis=1)


def emit_lower(done, get, u_ref):
    for i in range(4):
        wide = (i + 1) * TILE
        prod = dot_split((done[0][tile_at(i)], done[1][tile_at(i)]), (done[0][:wide], done[1][:wide]))
        for j in range(i + 1):
            u_ref[tri(i, j)] = get(i, j) - prod[:, tile_at(j)]


def spread_kernel(maps_ref, own_ref, sib_ref, s21, s22, dst):
    leaf, _ = places()
    row_lo = 4 + 4 * (leaf & 1)
    dst[...] = jnp.zeros_like(dst)
    for child, ref in ((leaf, own_ref), (leaf ^ 1, sib_ref)):
        scatter(dst, maps_ref, child, lambda i, j, ref=ref: ref[tile_at(i), tile_at(j)], range(8), row_lo)
    s21[...] = dst[:, :SEP]
    s22[...] = dst[:, SEP:]


def spread(maps, own, sib):
    return call(
        spread_kernel, "spread", 7, [maps, own, sib], [SMEM, vspec((UPD, UPD)), vspec((UPD, UPD))],
        [((SEP, SEP), F32), ((SEP, UPD), F32)], [VM((SEP, SEP + UPD), F32)],
    )


def solve_kernel_1(la, ta, lb, tb, s21, e0, e1, e2, e3, l21_ref, below_ref, x):
    _, y = places()
    x[...] = s21[...]
    for ref, rel in ((e0, 0), (e1, 3), (e2, 1), (e3, 2)):
        x[block((y + rel) & 3), :] += ref[...]
    solve_rows(lambda b: x[:, tile_at(b)], (la, ta, lb, tb), l21_ref)
    below_ref[...] = l21_ref[block(y), :]


def solve_1(factor, s21, pieces):
    return call(
        solve_kernel_1, "solve1", 4, [*factor, s21, *pieces],
        FACTOR + [vspec((SEP, SEP))] + [vspec((TILE, SEP))] * 4,
        [((SEP, SEP), F32), ((TILE, SEP), F32)], [VM((SEP, SEP), F32)],
    )


def diag_kernel_1(l21_ref, s22, g_ref, u_ref, e, t, sem):
    leaf, _ = places()
    at = pl.ds(pl.multiple_of((leaf & 1) * SEP, SEP), SEP)
    first = pltpu.make_async_copy(g_ref.at[:, :, at], e, sem.at[0])
    second = pltpu.make_async_copy(s22.at[:, at], t, sem.at[1])
    first.start()
    second.start()
    done = split(l21_ref[...])
    first.wait()
    second.wait()
    emit_lower(done, lambda i, j: e[i, :, tile_at(j)] + t[tile_at(i), tile_at(j)], u_ref)


def diag_1(l21, s22, g1):
    return call(
        diag_kernel_1, "diag1", 4, [l21, s22, g1], [vspec((SEP, SEP)), ANY, ANY],
        [(tiles_shape(10), F32)],
        [VM((4, TILE, SEP), F32), VM((SEP, SEP), F32), pltpu.SemaphoreType.DMA((2,))],
    )[0]


def cross_kernel_1(l21_ref, other_ref, s22, g_ref, u_ref, e, t, sem):
    leaf, _ = places()
    at = pl.ds(0, SEP)
    first = pltpu.make_async_copy(g_ref.at[:, :, at], e, sem.at[0])
    second = pltpu.make_async_copy(s22.at[:, at], t, sem.at[1])
    first.start()
    second.start()
    first.wait()
    second.wait()

    @pl.when((leaf & 1) == 1)
    def _():
        top = split(other_ref[...])
        for i in range(4):
            prod = dot_split(split(l21_ref[tile_at(i), :]), top)
            for j in range(4):
                u_ref[4 * i + j] = (e[i, :, tile_at(j)] + t[tile_at(i), tile_at(j)]) - prod[:, tile_at(j)]


def cross_1(l21, other, s22, g1):
    return call(
        cross_kernel_1, "cross1", 5, [l21, other, s22, g1], [vspec((SEP, SEP)), vspec((SEP, SEP)), ANY, ANY],
        [(tiles_shape(16), F32)],
        [VM((4, TILE, SEP), F32), VM((SEP, SEP), F32), pltpu.SemaphoreType.DMA((2,))],
    )[0]


def load_tiles(pairs, core, bufs, sem):
    for k, (pair, buf) in enumerate(zip(pairs, bufs)):
        for c in range(2):

            @pl.when(core == c)
            def _(pair=pair, buf=buf, c=c, k=k):
                pltpu.make_async_copy(pair[c], buf, sem.at[k]).start()

    return [pltpu.make_async_copy(pair[0], buf, sem.at[k]) for k, (pair, buf) in enumerate(zip(pairs, bufs))]


def load_rows_2(which, g_own, g_sw, e, sem, base):
    leaf, _ = places()
    core = leaf & 1
    z_rel = ((leaf >> 1) & 1) ^ which
    copies = []
    for y in range(4):
        for part in range(2):
            for src, who in ((g_own, core), (g_sw, 1 - core)):
                row = pl.multiple_of(who * 256 + y * 64, 64)
                dst = e.at[pl.ds(row, 64), part * SEP : (part + 1) * SEP]
                copies.append(pltpu.make_async_copy(src.at[y, z_rel, part * 64 : (part + 1) * 64], dst, sem.at[base + len(copies)]))
    for c in copies:
        c.start()
    return copies


def tile_getter(t11, tba, tbb):
    def get(i, j):
        if i < 4:
            return t11[tri(i, j)]
        if j < 4:
            return tba[4 * (i - 4) + j]
        return tbb[tri(i - 4, j - 4)]

    return get


def upper_kernel_2(maps_ref, la, ta, lb, tb, *refs):
    held, (g_own, g_sw, l21_ref, u_ref, half_ref, e, sem), bufs = refs[:12], refs[12:19], refs[19:]
    leaf, _ = places()
    core = leaf & 1
    copies = load_rows_2(0, g_own, g_sw, e, sem, 6)
    copies += load_tiles([(held[2 * k], held[2 * k + 1]) for k in range(6)], core, bufs, sem)
    for c in copies:
        c.wait()
    own = MAPS_AT[1] + (leaf >> 1)
    scatter(e, maps_ref, own, tile_getter(*bufs[:3]), range(7), 4)
    scatter(e, maps_ref, own ^ 1, tile_getter(*bufs[3:]), range(7), 4)
    done = solve_rows(lambda b: e[:, tile_at(b)], (la, ta, lb, tb), l21_ref)
    emit_lower(done, lambda i, j: e[tile_at(i), tile_at(4 + j)], u_ref)
    half_ref[...] = u_ref[pl.ds(core * 5, 5)]


def upper_2(maps, factor, held, g_own, g_sw):
    return call(
        upper_kernel_2, "upper2", 9, [maps, *factor, *held, g_own, g_sw],
        [SMEM] + FACTOR + [ANY] * 14,
        [((SEP, SEP), F32), (tiles_shape(10), F32), (tiles_shape(5), F32)],
        [VM((SEP, UPD), F32), pltpu.SemaphoreType.DMA((22,))] + [VM(tiles_shape(n), F32) for n in (10, 16, 10) * 2],
    )


def lower_kernel_2(maps_ref, la, ta, lb, tb, l21a, u10, *refs):
    held, (g_own, g_sw, mine_ref, send_ref, below_ref, e, l21b, u21, sem), bufs = refs[:8], refs[8:17], refs[17:]
    leaf, y = places()
    core = leaf & 1
    e[:, UPD:] = jnp.zeros((SEP, SEP), F32)
    copies = load_rows_2(1, g_own, g_sw, e, sem, 4)
    copies += load_tiles([(held[2 * k], held[2 * k + 1]) for k in range(4)], core, bufs, sem)
    for c in copies:
        c.wait()
    own = MAPS_AT[1] + (leaf >> 1)
    scatter(e, maps_ref, own, tile_getter(None, *bufs[:2]), range(4, 8), 8)
    scatter(e, maps_ref, own ^ 1, tile_getter(None, *bufs[2:]), range(4, 8), 8)
    done = solve_rows(lambda b: e[:, tile_at(b)], (la, ta, lb, tb), l21b)
    u21[...] = e[:, SEP:UPD] - dot_split(done, split(l21a[...]))
    child = MAPS_AT[2] + (leaf >> 2)
    stripe = pl.ds(pl.multiple_of(y * 32, 32), 32)
    for out_ref, who in ((mine_ref, leaf), (send_ref, leaf ^ 4)):
        out_ref[...] = jnp.zeros_like(out_ref)
        want = 4 + (who & 7)
        for j in range(1, 8):

            @pl.when(maps_ref[child, j] == want)
            def _(j=j, out_ref=out_ref):
                for c in range(min(j, 4)):
                    mj = maps_ref[child, c]

                    @pl.when(mj < 4)
                    def _(c=c, mj=mj):
                        if j < 4:
                            piece = u10[tri(j, c), stripe, :]
                        else:
                            row = pl.multiple_of((j - 4) * TILE + y * 32, 32)
                            piece = u21[pl.ds(row, 32), tile_at(c)]
                        out_ref[:, block(mj)] = piece

    pos = ((leaf & 3) * 4 + y) * 64

    @pl.when(pos < SEP)
    def _():
        below_ref[...] = l21a[pl.ds(pl.multiple_of(pos, 64), 64), :]

    @pl.when(pos >= SEP)
    def _():
        below_ref[...] = l21b[pl.ds(pl.multiple_of(pos - SEP, 64), 64), :]


def lower_2(maps, factor, l21a, u10, held, g_own, g_sw):
    return call(
        lower_kernel_2, "lower2", 9, [maps, *factor, l21a, u10, *held, g_own, g_sw],
        [SMEM] + FACTOR + [vspec((SEP, SEP)), vspec(tiles_shape(10))] + [ANY] * 10,
        [((32, SEP), F32), ((32, SEP), F32), ((64, SEP), F32)],
        [VM((SEP, SEP + UPD), F32), VM((SEP, SEP), F32), VM((SEP, SEP), F32), pltpu.SemaphoreType.DMA((20,))]
        + [VM(tiles_shape(n), F32) for n in (16, 10) * 2],
    )


def last_kernel(la, ta, lb, tb, e_ref, mine_ref, got_ref, out_ref):
    x = e_ref[...] + mine_ref[...] + got_ref[...]
    solve_rows(lambda b: x[:, tile_at(b)], (la, ta, lb, tb), out_ref)


def last(factor, rem3, mine, got):
    return call(
        last_kernel, "last", 3, [*factor, rem3, mine, got], FACTOR + [vspec((32, SEP))] * 3, [((32, SEP), F32)], []
    )[0]


def copy_kernel(plan, n_in, *refs):
    ins, outs = refs[:n_in], refs[n_in:]
    for src, src_at, dst, dst_at in plan:
        outs[dst][dst_at] = ins[src][src_at]


def copies(name, plan, ins, shapes, windows=None):
    windows = windows or [x.shape for x in ins]
    return call(
        functools.partial(copy_kernel, plan, len(ins)), name, 1, ins,
        [vspec(w) for w in windows], [(s, F32) for s in shapes], [],
    )


def flip(x, bits, cores=(0, 1)):
    n = lax.axis_size("leaf")
    return lax.ppermute(x, "leaf", [(i, i ^ bits) for i in range(n) if i % 2 in cores])


def swap(x, bit, cores=(0, 1)):
    return flip(x, 1 << bit, cores)


def shift(x, d):
    n = lax.axis_size("front")
    return lax.ppermute(x, "front", [(i, (i + d) % n) for i in range(n)])


def around(x):
    return [x, shift(x, 1), shift(x, -1), shift(x, 2)]


def after(x, *deps):
    return lax.optimization_barrier((x,) + deps)[0]


def body(leaf_update, sep1, rem1, sep2, rem2, sep3, rem3, map1, map2, map3):
    every = slice(None)
    whole = (every, every)
    at = lambda a, n: (slice(a, a + n), every)
    cut = lambda n, a=0, w=SEP: (slice(0, n), slice(a, a + w))
    maps = jnp.concatenate([map1, map2, map3], axis=0)
    e11_own, e21_own, s_own, e22_own, r2_own = copies(
        "cut",
        [(0, cut(64), 0, whole), (1, cut(128), 1, whole), (2, cut(32), 2, at(0, 32)), (3, cut(16), 2, at(32, 16)),
         (1, cut(128, SEP, UPD), 3, whole), (4, cut(64), 4, at(0, 64)), (4, cut(64, SEP), 4, at(64, 64))],
        [sep1, rem1, sep2, sep3, rem2], [(64, SEP), (128, SEP), (48, SEP), (128, UPD), (128, SEP)],
        [(64, SEP), (128, SEP + UPD), (32, SEP), (16, SEP), (64, UPD)],
    )
    e11 = around(e11_own)
    s_sib = swap(s_own, 1)
    u_sib = swap(leaf_update, 0)
    g1 = lax.all_gather(e22_own, "front", axis=0, tiled=False)
    s21, s22 = spread(maps, leaf_update, u_sib)
    e11[1] = after(e11[1], s_sib)
    e11 = copies("join1", [(k, every, 0, at(64 * k, 64)) for k in range(4)], e11, [(256, SEP)])[0]
    e11_sw = swap(e11, 0)
    e21_own = copies(
        "join2", [(0, whole, 0, at(0, 128)), (1, whole, 0, at(128, 48)), (2, whole, 0, at(176, 48))],
        [e21_own, s_own, after(s_sib, e11)], [(224, SEP)],
    )[0]
    e21 = around(e21_own)
    r2_sib = swap(after(r2_own, e11), 1)
    e11 = after(e11, s21)
    la, ta, fs, head = pivot_head(1, maps, [e11, e11_sw], [leaf_update, u_sib], [(SEP, SEP)] * 2)
    r2_sib, e21[1], e21[2] = lax.optimization_barrier((r2_sib, e21[1], e21[2], ta))[:3]
    r2 = copies(
        "join3", [(0, whole, 0, (0, every, every)), (1, whole, 0, (1, every, every))], [r2_own, r2_sib], [(2, 128, SEP)]
    )[0]
    g2 = lax.all_gather(r2, "front", axis=0, tiled=False)
    lb, tb, out_p1 = pivot_tail(1, fs, head)
    e21[3] = after(e21[3], tb)
    l21, out_b1 = solve_1((la, ta, lb, tb), s21, e21)
    other = swap(l21, 0)
    uhh = diag_1(l21, s22, after(g1, l21))
    z11 = swap(uhh, 1, (0,))
    uhh_sw = swap(uhh, 0)
    uba = cross_1(l21, after(other, uhh), s22, g1)
    s3, t3 = copies(
        "join4",
        [(k, at(128, 96), 0, at(96 * k, 96)) for k in range(4)]
        + [(k, at(160 + 48 * z, 16), 1, at(32 * k + 16 * z, 16)) for k in range(4) for z in range(2)],
        [after(e21[0], uba)] + e21[1:], [(384, SEP), (128, SEP)],
    )
    s3_sw = swap(s3, 0)
    z11 = after(z11, s3)
    z11_sw = swap(z11, 0)
    uba_sw = swap(uba, 0)
    zbb = swap(after(uhh, z11), 1, (1,))
    zba = swap(after(uba, z11), 1, (1,))
    la, ta, fs, head = pivot_head(2, maps, [s3, s3_sw], [uhh, uhh_sw, z11, z11_sw], [tiles_shape(10)] * 4)
    g2_sw = swap(after(g2, ta), 0)
    t3z = swap(after(t3, ta), 2)
    lb, tb, out_p2 = pivot_tail(2, fs, head)
    zbb, zba, t3z = lax.optimization_barrier((zbb, zba, t3z, tb))[:3]
    factor = (la, ta, lb, tb)
    zbb_sw = swap(zbb, 0)
    zba_sw = swap(zba, 0)
    held = [uhh, uhh_sw, uba_sw, uba, uhh_sw, uhh, z11, z11_sw, zba_sw, zba, zbb_sw, zbb]
    l21a, v10, half = upper_2(maps, factor, held, g2, g2_sw)
    half_z = swap(half, 2)
    t3z_sw = swap(after(t3z, half), 0)
    mine, send, out_b2 = lower_2(maps, factor, l21a, v10, held[2:6] + held[8:], g2, g2_sw)
    half_z = after(half_z, mine)
    half_sw = swap(half_z, 0)
    got = swap(send, 2)
    s3 = [s3, s3_sw, t3z, t3z_sw]
    la, ta, fs, head = pivot_head(3, maps, s3, [v10, half_z, half_sw], [tiles_shape(n) for n in (10, 5, 5)])
    lb, tb, out_p3 = pivot_tail(3, fs, head)
    out_b3 = last((la, ta, lb, tb), rem3, mine, after(got, tb))
    return out_p1, out_b1, out_p2, out_b2, out_p3, out_b3


def solution(mesh):
    both = P(("leaf", "front"), None)
    in_specs = (P("leaf", None),) + (both,) * 6 + (P(), P(), P())
    return jax.shard_map(body, mesh=mesh, in_specs=in_specs, out_specs=(both,) * 6, check_vma=False)
```
